32 devices in a mesh: runs: 2 (over x), slab: 16 (over z, y, core).
Axes of the slice: x: 2, y: 2, z: 4, core: 2. Of those that a mesh axis runs over, the one named last changes fastest.
Arguments:
- positions: float32 [3, 4096, 128], P(None, ('runs', 'slab')), parts along dimension 1, may hold values from 0 to 16, as said below
- velocity: float32 [3, 4096, 128], P(None, ('runs', 'slab')), parts along dimension 1, may hold values from -3 to 3
- density: float32 [4096, 128], P(('runs', 'slab')), parts along dimension 0, may hold values from 0.97 to 1.03
- mass: float32 [4096, 128], P(('runs', 'slab')), parts along dimension 0, may hold values from 0.005 to 0.012
- walls: int32 [4096, 128], P(('runs', 'slab')), parts along dimension 0, may hold values 0 or 1
- pairs: int32 [2, 50624], P(None, ('runs', 'slab')), parts along dimension 1, may hold values from 0 to 255, as said below
- counts: int32 [32], P(('runs', 'slab')), parts along dimension 0, may hold values from 1 to 1582, as said below
Outputs:
- new_offsets: float32 [3, 4096, 128], P(None, ('runs', 'slab')), parts along dimension 1
- new_velocity: float32 [3, 4096, 128], P(None, ('runs', 'slab')), parts along dimension 1
- new_density: float32 [4096, 128], P(('runs', 'slab')), parts along dimension 0
The draws below stay inside these ranges and needn't reach their ends.
There are 2 independent parts, one for each index of `runs`. The reference program is written for one: setup_inputs(seed, part) draws one part's arguments, and reference() takes and returns one part's arrays. A program takes and returns all parts, laid end to end along the dimension named above; each array names one. Nothing has to cross between parts.
Inputs may be any that keep to these rules, and one draw needn't show every extreme that they name: `positions`: cell c = s*128 + y*16 + z of slab s: its particles have first coordinate in [s, s+1), second in [y, y+1), third in [z, z+1). `pairs`: within a slab's count, entries naming a cell of the next slab come after all others; the last slab has none; no unordered cell pair appears twice; entries past the count are (0, 0). Only cells whose particles can lie within distance 2h are paired. `counts`: some slab's count is 1582.
All inputs are finite; a program needn't handle non-finite values. No bound on the sum of `walls` on one device may be relied on, other than what follows from the above.
Results may differ from the reference program's by a relative error of at most 0.0003.
Values sent between devices are 32-bit elements; how exact they have to be, the bound alone decides.
No kernel may reach another device: no remote copies, remote signals or barrier semaphores. Data moves between devices by JAX's collectives and lax.ppermute only.
A program may use at most 64 MiB of HBM per device.

```python
import math
import jax
import jax.numpy as jnp
import numpy as np
from jax import lax

PARTICLES = 128
GY = 8
GZ = 16
CELLS = 128
PAIRS_DEV = 1582
CELLS_ALL = 2048
N_SLAB = 16


def cell_table():
    entries = []
    for row_y in range(GY):
        for layer_z in range(GZ):
            home_cell = row_y * GZ + layer_z
            entries.append((home_cell, home_cell, layer_z, layer_z, 0))
            if layer_z + 1 < GZ:
                entries.append((home_cell, home_cell + 1, layer_z, layer_z + 1, 0))
            for shift_z in (-1, 0, 1):
                other_z = layer_z + shift_z
                if row_y + 1 < GY and 0 <= other_z < GZ:
                    entries.append((home_cell, (row_y + 1) * GZ + other_z, layer_z, other_z, 0))
            for shift_y in (-1, 0, 1):
                for shift_z in (-1, 0, 1):
                    other_y = row_y + shift_y
                    other_z = layer_z + shift_z
                    if 0 <= other_y < GY and 0 <= other_z < GZ:
                        entries.append((home_cell, CELLS + other_y * GZ + other_z, layer_z, other_z, 1))
    return np.array(entries, dtype=np.int32)


def pair_lists(key):
    table = cell_table()
    first_cell = jnp.asarray(table[:, 0])
    second_cell = jnp.asarray(table[:, 1])
    first_layer = jnp.asarray(table[:, 2])
    second_layer = jnp.asarray(table[:, 3])
    crossing = jnp.asarray(table[:, 4])
    key_height, key_full, key_order = jax.random.split(jax.random.fold_in(key, 11), 3)
    lowest = max(1, GZ // 4)
    heights = jax.random.randint(key_height, (N_SLAB,), lowest, GZ + 1)
    chosen = jax.random.randint(key_full, (), 0, N_SLAB - 1)
    slab_ids = jnp.arange(N_SLAB, dtype=jnp.int32)
    heights = jnp.where((slab_ids == chosen) | (slab_ids == chosen + 1), GZ, heights).astype(jnp.int32)
    next_heights = jnp.concatenate([heights[1:], jnp.zeros((1,), jnp.int32)])
    second_limit = jnp.where(crossing[None, :] == 1, next_heights[:, None], heights[:, None])
    alive_mask = (first_layer[None, :] < heights[:, None]) & (second_layer[None, :] < second_limit)
    order_keys = jax.random.split(key_order, N_SLAB)
    shuffled = jax.vmap(lambda item: jax.random.permutation(item, PAIRS_DEV))(order_keys).astype(jnp.int32)
    sort_key = (1 - alive_mask.astype(jnp.int32)) * (2 * PAIRS_DEV) + crossing[None, :] * PAIRS_DEV + shuffled
    order = jnp.argsort(sort_key, axis=1, stable=True)
    alive_sorted = jnp.take_along_axis(alive_mask, order, axis=1)
    first_sorted = jnp.where(alive_sorted, jnp.take(first_cell, order), 0)
    second_sorted = jnp.where(alive_sorted, jnp.take(second_cell, order), 0)
    lists = jnp.stack([first_sorted, second_sorted]).reshape(2, N_SLAB * PAIRS_DEV).astype(jnp.int32)
    totals = jnp.sum(alive_mask.astype(jnp.int32), axis=1).astype(jnp.int32)
    return (lists, totals)


def draw_pairs(key, part):
    return pair_lists(key)[0]


def draw_counts(key, part):
    return pair_lists(key)[1]


def draw_positions(key, part):
    cell_ids = jnp.arange(CELLS_ALL, dtype=jnp.int32)
    slab_of = (cell_ids // CELLS).astype(jnp.float32)
    within = cell_ids % CELLS
    row_of = (within // GZ).astype(jnp.float32)
    layer_of = (within % GZ).astype(jnp.float32)
    corner = jnp.stack([slab_of, row_of, layer_of])[:, :, None]
    jitter = jax.random.uniform(jax.random.fold_in(key, 5), (3, CELLS_ALL, PARTICLES), jnp.float32, 0.0, 0.999)
    return (corner + jitter).astype(jnp.float32)


def place_ends(drawn, own_key, least, largest):
    shape = drawn.shape
    place = [jax.random.randint(jax.random.fold_in(own_key, axis), (), 0, shape[axis]) for axis in range(len(shape))]
    drawn = drawn.at[tuple(place)].set(least)
    longest = shape.index(max(shape))
    place[longest] = (place[longest] + 1) % shape[longest]
    return drawn.at[tuple(place)].set(largest)


def steps_of(rng, shape, shards, least, top_value):
    gain, own = 1.0, jax.random.fold_in(rng, 6)
    for axis_at, blocks in shards:
        steps = jnp.exp(jax.random.uniform(jax.random.fold_in(own, axis_at), (blocks,), jnp.float32, least / len(shards), top_value / len(shards)))
        gain = gain * jnp.repeat(steps, shape[axis_at] // blocks).reshape([-1 if axis == axis_at else 1 for axis in range(len(shape))])
    return gain


def bell_draw(stream_key, shape, scale, most, cuts=(), held_as=jnp.bfloat16):
    values = jax.random.normal(stream_key, shape, jnp.float32) * scale
    if len(cuts) > 0:
        values = steps_of(stream_key, shape, cuts, -0.22, 0.18) * values
    return jnp.clip(values, min=-most, max=most).astype(held_as)


def setup_inputs(seed: int = 0, part: int = 0) -> dict:
    arg_keys = jax.random.split(jax.random.key(seed), 8)
    part_keys = jax.random.split(jax.random.fold_in(arg_keys[7], part), 8)
    return {
        "positions": draw_positions(jax.random.fold_in(jax.random.fold_in(arg_keys[7], part), 71), part),
        "velocity": bell_draw(part_keys[1], (3, CELLS_ALL, PARTICLES), 0.5, 3.0, ((1, 16),), jnp.float32),
        "density": jnp.clip(0.97 + 0.059999943 * jax.random.uniform(part_keys[2], (CELLS_ALL, PARTICLES), jnp.float32) ** steps_of(part_keys[2], (CELLS_ALL, PARTICLES), ((0, 16),), -0.2, 0.2), 0.97, 1.03),
        "mass": jnp.clip(jnp.exp(math.log(0.012) - 0.8754688 * jax.random.uniform(part_keys[3], (CELLS_ALL, PARTICLES), jnp.float32) ** steps_of(part_keys[3], (CELLS_ALL, PARTICLES), ((0, 16),), -0.2, 0.2)), 0.005, 0.012),
        "walls": place_ends((jax.random.randint(part_keys[4], (CELLS_ALL, PARTICLES), 0, 8) < 1).astype(jnp.int32), jax.random.fold_in(part_keys[4], 1), 0, 1),
        "pairs": draw_pairs(jax.random.fold_in(jax.random.fold_in(arg_keys[7], part), 71), part),
        "counts": draw_counts(jax.random.fold_in(jax.random.fold_in(arg_keys[7], part), 71), part),
    }


SMOOTH = 0.5
SOUND = 10.0
RHO_REST = 1.0
BETA = 1.0
DIFFUSE = 0.5
CFL_NUMBER = 0.25
GRAD_SCALE = -105.0 / (16.0 * math.pi * SMOOTH ** 5)
group_blocks = 16

def tait_pressure(density):
    ratio = density / RHO_REST
    square = ratio * ratio
    return SOUND * SOUND * RHO_REST / 7.0 * (square * square * square * ratio - 1.0)

def block_terms(home_src, home_pres, away_src, away_pres, weights):
    home_pos = home_src[0:3]
    home_vel = home_src[3:6]
    home_rho = home_src[6][:, :, None]
    home_mass = home_src[7][:, :, None]
    away_pos = away_src[0:3]
    away_vel = away_src[3:6]
    away_rho = away_src[6][:, None, :]
    away_mass = away_src[7][:, None, :]
    rel_pos = home_pos[:, :, :, None] - away_pos[:, :, None, :]
    rel_vel = home_vel[:, :, :, None] - away_vel[:, :, None, :]
    scale_w = weights[:, None, None]
    dist_sq = lax.optimization_barrier(jnp.sum(rel_pos * rel_pos, axis=0))
    shell = jnp.maximum(1.0 - 0.5 * jnp.sqrt(dist_sq) / SMOOTH, 0.0)
    kernel_slope = GRAD_SCALE * shell * shell * shell
    closing = lax.optimization_barrier(jnp.sum(rel_vel * rel_pos, axis=0))
    star_pressure = 0.5 * (home_pres[:, :, None] + away_pres[:, None, :]) + 0.25 * BETA * SOUND * (home_rho + away_rho) * jnp.maximum(-closing / SMOOTH, 0.0)
    push_term = scale_w * 2.0 * star_pressure / (home_rho * away_rho) * kernel_slope
    force_home = -lax.optimization_barrier(jnp.sum(away_mass * push_term * rel_pos, axis=3))
    force_away = lax.optimization_barrier(jnp.sum(home_mass * push_term * rel_pos, axis=2))
    diverge = kernel_slope * closing
    diffuse_shape = kernel_slope * dist_sq / (dist_sq + 0.01 * SMOOTH * SMOOTH)
    rate_home = lax.optimization_barrier(jnp.sum(scale_w * away_mass * (home_rho / away_rho * diverge + 2.0 * DIFFUSE * (away_rho - home_rho) / away_rho * diffuse_shape), axis=2))
    rate_away = lax.optimization_barrier(jnp.sum(scale_w * home_mass * (away_rho / home_rho * diverge + 2.0 * DIFFUSE * (home_rho - away_rho) / home_rho * diffuse_shape), axis=1))
    return (jnp.concatenate([force_home, rate_home[None]], 0), jnp.concatenate([force_away, rate_away[None]], 0))

def accumulate(totals, source, source_pres, padded, start_at, stop_at):
    cell_limit = source.shape[1]

    def turn(turn_index, running):
        columns = lax.dynamic_slice_in_dim(padded, turn_index * group_blocks, group_blocks, 1)
        position = turn_index * group_blocks + jnp.arange(group_blocks, dtype=jnp.int32)
        alive = (position >= start_at) & (position < stop_at)
        home_cell = columns[0]
        away_cell = jnp.minimum(columns[1], cell_limit - 1)
        weights = jnp.where(alive, jnp.where(home_cell == columns[1], 0.5, 1.0), 0.0).astype(jnp.float32)
        terms_home, terms_away = block_terms(jnp.take(source, home_cell, axis=1), jnp.take(source_pres, home_cell, axis=0), jnp.take(source, away_cell, axis=1), jnp.take(source_pres, away_cell, axis=0), weights)
        running = running.at[:, home_cell].add(terms_home)
        return running.at[:, away_cell].add(terms_away)
    return lax.fori_loop(start_at // group_blocks, (stop_at + group_blocks - 1) // group_blocks, turn, totals)

def reference(positions, velocity, density, mass, walls, pairs, counts):
    state = jnp.concatenate([positions, velocity, density[None], mass[None]], 0).reshape(8, N_SLAB, CELLS, PARTICLES)
    pressure = tait_pressure(density).reshape(N_SLAB, CELLS, PARTICLES)
    extra = -PAIRS_DEV % group_blocks
    pair_dev = jnp.pad(pairs.reshape(2, N_SLAB, PAIRS_DEV), ((0, 0), (0, 0), (0, extra)))

    def per_device(device):
        own_state = lax.dynamic_index_in_dim(state, device, 1, keepdims=False)
        own_pres = lax.dynamic_index_in_dim(pressure, device, 0, keepdims=False)
        follower = jnp.minimum(device + 1, N_SLAB - 1)
        present = (device < N_SLAB - 1).astype(jnp.float32)
        neighbour = lax.dynamic_index_in_dim(state, follower, 1, keepdims=False) * present
        source = jnp.concatenate([own_state, neighbour], 1)
        source_pres = jnp.concatenate([own_pres, tait_pressure(neighbour[6])], 0)
        columns = lax.dynamic_index_in_dim(pair_dev, device, 1, keepdims=False)
        total_count = lax.dynamic_index_in_dim(counts, device, 0, keepdims=False)
        empty = jnp.zeros((4, 2 * CELLS, PARTICLES), jnp.float32)
        return accumulate(empty, source, source_pres, columns, jnp.int32(0), total_count)
    totals = lax.map(per_device, jnp.arange(N_SLAB, dtype=jnp.int32))
    shifted = jnp.concatenate([jnp.zeros((1, 4, CELLS, PARTICLES), jnp.float32), totals[:-1, :, CELLS:]], 0)
    summed = jnp.transpose(totals[:, :, :CELLS] + shifted, (1, 0, 2, 3)).reshape(4, CELLS_ALL, PARTICLES)
    fastest = jnp.max(lax.optimization_barrier(jnp.sum(velocity * velocity, axis=0)))
    step_size = CFL_NUMBER * SMOOTH / (SOUND + jnp.sqrt(fastest))
    gravity = jnp.array([0.0, 0.0, -9.81], jnp.float32)[:, None, None]
    fluid = (walls == 0)[None]
    new_velocity = jnp.where(fluid, velocity + step_size * (summed[:3] + gravity), velocity)
    cell_ids = jnp.arange(CELLS_ALL, dtype=jnp.int32)
    within = cell_ids % CELLS
    corner = jnp.stack([(cell_ids // CELLS).astype(jnp.float32), (within // GZ).astype(jnp.float32), (within % GZ).astype(jnp.float32)])[:, :, None]
    offsets = positions - corner
    new_offsets = jnp.where(fluid, offsets + step_size * new_velocity, offsets)
    new_density = density + step_size * summed[3]
    return (new_offsets, new_velocity, new_density)
```

```python
import math, functools
import jax, jax.numpy as jnp
from jax import lax
from jax.experimental import pallas as pl
from jax.experimental.pallas import tpu as pltpu
bf=jnp.bfloat16; f32=jnp.float32
SMOOTH=0.5; GS=-105.0/(16.0*math.pi*SMOOTH**5); ETA=0.01*SMOOTH*SMOOTH
K=48
def split3(t):
    a=t.astype(bf).astype(f32); r=t-a; b=r.astype(bf).astype(f32); c=(r-b).astype(bf).astype(f32)
    return a,b,c
def tait(d):
    s=d*d; return 100.0/7.0*(s*s*s*d-1.0)
def prep(c,state,fa,fb,col,w16,home):
    T=state[c]
    io=lax.broadcasted_iota(jnp.int32,(8,128),0)
    x,y,z,vx,vy,vz,rho,m=[T[k:k+1] for k in range(8)]
    bc=lambda r: jnp.broadcast_to(r,(8,128))
    xn=split3(bc(x*x+y*y+z*z)); mm=split3(bc(x*vx+y*vy+z*vz))
    t=split3(T)
    vel=pltpu.roll(T,5,0)
    vx_=split3(jnp.where(io<3,vel,pltpu.roll(T,3,0)))
    order=[(0,0),(0,1),(1,0),(1,1),(0,2),(2,0)]
    one=jnp.ones((8,128),f32); zero=jnp.zeros((8,128),f32)
    sl=[(one,xn[0],-0.5*mm[0]),(one,xn[1],-0.5*mm[1]),(one,xn[2],-0.5*mm[2])]
    sl+=[(xn[i],one,zero) for i in range(3)]
    sl+=[(mm[i],zero,-0.5*one) for i in range(3)]
    sl+=[(zero,zero,zero)]*3
    L=[];D=[];N=[]
    for g,(p,q) in enumerate(order):
        s6,s7=sl[2*g],sl[2*g+1]
        L.append(jnp.where(io<6,t[p],jnp.where(io==6,s6[0],s7[0])))
        D.append(jnp.where(io<3,-2.0*t[q],jnp.where(io<6,0.0,jnp.where(io==6,s6[1],s7[1]))))
        N.append(jnp.where(io<6,0.5*vx_[q],jnp.where(io==6,s6[2],s7[2])))
    fb[c,:,:128]=jnp.concatenate(D,0).astype(bf)
    fb[c,:,128:]=jnp.concatenate(N,0).astype(bf)
    P=tait(rho)
    ext=jnp.where(io==0,bc(20.0*rho),jnp.where(io==1,bc(P),0.0))
    if home:
        L.append(ext); L.append(zero)
        tr=jnp.transpose(jnp.concatenate(L,0))
        fa[c]=tr[:,:K].astype(bf)
        col[c]=tr[:,K:K+8]
    V=GS*m/rho
    i16=lax.broadcasted_iota(jnp.int32,(16,128),0)
    b16=lambda r: jnp.broadcast_to(r,(16,128))
    base=b16(V)*jnp.where(i16<3,1.0,jnp.where(i16<6,b16(x),jnp.where(i16<9,b16(y),b16(z))))
    s=split3(base); md=i16%3
    wu=jnp.where(i16<12,jnp.where(md==0,s[0],jnp.where(md==1,s[1],s[2])),0.0)
    v2=split3(b16(V*(-1.0/20.0)))
    wa=jnp.where(i16==12,v2[0],jnp.where(i16==13,v2[1],0.0))
    w16[c,:,:128]=wu.astype(bf); w16[c,:,128:]=wa.astype(bf)
    return ext
def dotn(a,b): return lax.dot_general(a,b,(((1,),(0,)),((),())),preferred_element_type=f32)
def dott(a,b): return lax.dot_general(a,b,(((1,),(1,)),((),())),preferred_element_type=f32)
def pairvals(dn,colv,rowv):
    d=jnp.maximum(dn[:,:128],1e-12); nch=dn[:,128:]
    ra=colv[:,0:1]; pa=colv[:,1:2]; rb=rowv[0:1]; pb=rowv[1:2]
    q=d*lax.rsqrt(d); s=jnp.maximum(1.0-q,0.0); s3=s*s*s
    nc2=nch*(ra+rb)
    u=s3*((pa+pb)+jnp.maximum(nc2,0.0))
    yy=lax.rsqrt(d+ETA); psi=d*yy*yy
    z=s3*nc2; wv=(rb-ra)*s3*(psi+nch)
    return u.astype(bf),(z-wv).astype(bf),(z+wv).astype(bf)
def kern(G,home_ref,away_ref,cnt_ref,state,out,fa,fb,col,row,w16,R):
    ncell=state.shape[0]
    R[...]=jnp.zeros_like(R)
    def pro(c,_):
        row[c]=prep(c,state,fa,fb,col,w16,True); return _
    lax.fori_loop(0,ncell,pro,0)
    cnt=cnt_ref[0]
    def body(t,_):
        res=[]
        for g in range(G):
            k=t*G+g
            i=home_ref[k]; j=away_ref[k]
            dn=dotn(fa[i],fb[j])
            u,A,B=pairvals(dn,col[i],row[j])
            rh=dott(w16[j],jnp.concatenate([u,A],1))
            ra=dotn(w16[i],jnp.concatenate([u,B],0))
            wt=jnp.where(k<cnt,jnp.where(i==j,0.5,1.0),0.0).astype(f32)
            res.append((i,j,wt,rh,ra))
        for i,j,wt,rh,ra in res:
            R[i]+=wt*rh
            R[j]+=wt*ra
        return _
    lax.fori_loop(0,(cnt+G-1)//G,body,0)
    def epi(c,_):
        r=R[c]; T=state[c]; rho=T[6:7]
        r0=r[0:1]+r[1:2]+r[2:3]
        outs=[]
        for k in range(3):
            rx=r[3+3*k:4+3*k]+r[4+3*k:5+3*k]+r[5+3*k:6+3*k]
            out[c,k:k+1]=(rx-T[k:k+1]*r0)/rho
        out[c,3:4]=r[12:13]+r[13:14]
        return _
    lax.fori_loop(0,ncell,epi,0)
def call(G,home,away,cnt,state):
    nc=state.shape[0]
    return pl.pallas_call(functools.partial(kern,G),
      out_shape=jax.ShapeDtypeStruct((nc,4,128),f32),
      in_specs=[pl.BlockSpec(memory_space=pltpu.SMEM)]*3+[pl.BlockSpec(memory_space=pltpu.VMEM)],
      out_specs=pl.BlockSpec(memory_space=pltpu.VMEM),
      scratch_shapes=[pltpu.VMEM((nc,128,K),bf),pltpu.VMEM((nc,K,256),bf),pltpu.VMEM((nc,128,8),f32),pltpu.VMEM((nc,8,128),f32),pltpu.VMEM((nc,16,256),bf),pltpu.VMEM((nc,16,128),f32)],
      compiler_params=pltpu.CompilerParams(vmem_limit_bytes=60<<20))(home,away,cnt,state)


from jax.sharding import PartitionSpec as PS

GZ = 16
CFL_NUMBER = 0.25
SOUND = 10.0
GROUP = 8


def shift(array, by):
    peers = lax.axis_size("slab")
    return lax.ppermute(array, "slab", [(i, i + by) for i in range(peers) if 0 <= i + by < peers])


def per_device(positions, velocity, density, mass, walls, pairs, counts):
    cells = density.shape[0]
    slots = pairs.shape[1]
    slab = lax.axis_index("slab").astype(jnp.float32)
    middle = jnp.stack([slab + 1.0, jnp.float32(4.0), jnp.float32(8.0)])[:, None, None]
    state = jnp.concatenate([positions - middle, velocity, density[None], mass[None]], 0)
    state = jnp.transpose(state, (1, 0, 2))
    arrived = shift(state, -1)
    one_over = (jnp.arange(8) == 0).astype(jnp.float32)[None, :, None]
    source = jnp.concatenate([state, arrived + one_over], 0)
    fastest = lax.pmax(jnp.max(jnp.sum(velocity * velocity, axis=0)), "slab")
    step_size = CFL_NUMBER * SMOOTH / (SOUND + jnp.sqrt(fastest))
    extra = -slots % GROUP
    home = jnp.pad(jnp.minimum(pairs[0], pairs[1]), (0, extra))
    away = jnp.pad(jnp.maximum(pairs[0], pairs[1]), (0, extra))
    totals = call(GROUP, home, away, counts, source)
    returned = shift(totals[cells:], 1)
    summed = jnp.transpose(totals[:cells] + returned, (1, 0, 2))
    gravity = jnp.array([0.0, 0.0, -9.81], jnp.float32)[:, None, None]
    fluid = (walls == 0)[None]
    new_velocity = jnp.where(fluid, velocity + step_size * (summed[:3] + gravity), velocity)
    within = jnp.arange(cells, dtype=jnp.int32)
    corner = jnp.stack(
        [
            jnp.zeros((cells,), jnp.float32) + slab,
            (within // GZ).astype(jnp.float32),
            (within % GZ).astype(jnp.float32),
        ]
    )[:, :, None]
    offsets = positions - corner
    new_offsets = jnp.where(fluid, offsets + step_size * new_velocity, offsets)
    new_density = density + step_size * summed[3]
    return (new_offsets, new_velocity, new_density)


def solution(mesh):
    wide = PS(None, ("runs", "slab"), None)
    flat = PS(("runs", "slab"), None)
    return jax.shard_map(
        per_device,
        mesh=mesh,
        in_specs=(wide, wide, flat, flat, flat, PS(None, ("runs", "slab")), PS(("runs", "slab"))),
        out_specs=(wide, wide, flat),
        check_vma=False,
    )
```

```python
import math, functools
import jax, jax.numpy as jnp
from jax import lax
from jax.experimental import pallas as pl
from jax.experimental.pallas import tpu as pltpu
bf=jnp.bfloat16; f32=jnp.float32
SMOOTH=0.5; GS=-105.0/(16.0*math.pi*SMOOTH**5); ETA=0.01*SMOOTH*SMOOTH
K=48
def split3(t):
    a=t.astype(bf).astype(f32); r=t-a; b=r.astype(bf).astype(f32); c=(r-b).astype(bf).astype(f32)
    return a,b,c
def tait(d):
    s=d*d; return 100.0/7.0*(s*s*s*d-1.0)
def prep(c,state,fa,fb,col,w16,home):
    T=state[c]
    io=lax.broadcasted_iota(jnp.int32,(8,128),0)
    x,y,z,vx,vy,vz,rho,m=[T[k:k+1] for k in range(8)]
    bc=lambda r: jnp.broadcast_to(r,(8,128))
    xn=split3(bc(x*x+y*y+z*z)); mm=split3(bc(x*vx+y*vy+z*vz))
    t=split3(T)
    vel=pltpu.roll(T,5,0)
    vx_=split3(jnp.where(io<3,vel,pltpu.roll(T,3,0)))
    order=[(0,0),(0,1),(1,0),(1,1),(0,2),(2,0)]
    one=jnp.ones((8,128),f32); zero=jnp.zeros((8,128),f32)
    sl=[(one,xn[0],-0.5*mm[0]),(one,xn[1],-0.5*mm[1]),(one,xn[2],-0.5*mm[2])]
    sl+=[(xn[i],one,zero) for i in range(3)]
    sl+=[(mm[i],zero,-0.5*one) for i in range(3)]
    sl+=[(zero,zero,zero)]*3
    L=[];D=[];N=[]
    for g,(p,q) in enumerate(order):
        s6,s7=sl[2*g],sl[2*g+1]
        L.append(jnp.where(io<6,t[p],jnp.where(io==6,s6[0],s7[0])))
        D.append(jnp.where(io<3,-2.0*t[q],jnp.where(io<6,0.0,jnp.where(io==6,s6[1],s7[1]))))
        N.append(jnp.where(io<6,0.5*vx_[q],jnp.where(io==6,s6[2],s7[2])))
    fb[c,0]=jnp.concatenate(D,0).astype(bf)
    fb[c,1]=jnp.concatenate(N,0).astype(bf)
    P=tait(rho)
    ext=jnp.where(io==0,bc(20.0*rho-20.0),jnp.where(io==1,bc(P),bc(20.0*rho+20.0)))
    if home:
        L.append(ext); L.append(zero)
        tr=jnp.transpose(jnp.concatenate(L,0))
        fa[c]=tr[:,:K].astype(bf)
        col[c,0]=jnp.broadcast_to(tr[:,K:K+1],(128,128)); col[c,1]=jnp.broadcast_to(tr[:,K+1:K+2],(128,128))
    V=GS*m/rho
    i16=lax.broadcasted_iota(jnp.int32,(16,128),0)
    b16=lambda r: jnp.broadcast_to(r,(16,128))
    base=b16(V)*jnp.where(i16<3,1.0,jnp.where(i16<6,b16(x),jnp.where(i16<9,b16(y),b16(z))))
    s=split3(base); md=i16%3
    wu=jnp.where(i16<12,jnp.where(md==0,s[0],jnp.where(md==1,s[1],s[2])),0.0)
    v2=split3(b16(V*(-1.0/20.0)))
    wa=jnp.where(i16==12,v2[0],jnp.where(i16==13,v2[1],0.0))
    w16[c,0]=wu.astype(bf); w16[c,1]=wa.astype(bf)
    return ext
def dotn(a,b): return lax.dot_general(a,b,(((1,),(0,)),((),())),preferred_element_type=f32)
def dott(a,b): return lax.dot_general(a,b,(((1,),(1,)),((),())),preferred_element_type=f32)

F={'nb4','pu8'}
def kern(G,NB,home_ref,away_ref,cnt_ref,state,out,fa,fb,col,row,w16,R,db):
    ncell=state.shape[0]
    R[...]=jnp.zeros_like(R)
    UP=PU
    own=ncell//2
    def pro_home(c,_):
        for u in range(UP):
            e=c*UP+u
            row[e]=prep(e,state,fa,fb,col,w16,True)
        return _
    def pro_away(c,_):
        for u in range(UP):
            e=c*UP+u
            row[e]=prep(e,state,fa,fb,col,w16,False)
        return _
    lax.fori_loop(0,own//UP,pro_home,0)
    both=cnt_ref[1]>0
    @pl.when(both)
    def _(): lax.fori_loop(own//UP,ncell//UP,pro_home,0)
    @pl.when(jnp.logical_not(both))
    def _(): lax.fori_loop(own//UP,ncell//UP,pro_away,0)
    cnt=cnt_ref[0]
    def sa(k,b):
        i=home_ref[k]; j=away_ref[k]
        dn=dotn(fa[i],jnp.concatenate([fb[j,0],fb[j,1]],1))
        db[b,0]=dn[:,:128]; db[b,1]=dn[:,128:]
    def sv(k,b):
        i=home_ref[k]; j=away_ref[k]
        d=jnp.maximum(db[b,0],1e-12); nch=db[b,1]
        rb=row[j,0:1]; pb=row[j,1:2]; rb40=row[j,2:3]
        ra=col[i,0]; pa=col[i,1]
        q=d*lax.rsqrt(d); s=jnp.maximum(1.0-q,0.0); s3=(s*s)*s
        nc2=nch*(ra+rb40)
        u=(s3*((pa+pb)+jnp.maximum(nc2,0.0))).astype(bf)
        dd=d.astype(bf); s3=s3.astype(bf); nc2=nc2.astype(bf); nch=nch.astype(bf)
        psi=dd/(dd+jnp.bfloat16(ETA))
        X=(rb.astype(bf)-ra.astype(bf))*(psi+nch)
        return u,s3*(nc2-X),s3*(nc2+X)
    def sbc(k,uab):
        u,A,B=uab
        i=home_ref[k]; j=away_ref[k]
        if 'b2' in F:
            r2=dott(w16[j,0],jnp.concatenate([u,A],0)); rh=r2[:,:128]+r2[:,128:]
        else: rh=dott(jnp.concatenate([w16[j,0],w16[j,1]],1),jnp.concatenate([u,A],1))
        if 'c2' in F:
            r2=dotn(w16[i,0],jnp.concatenate([u,B],1)); ra=r2[:,:128]+r2[:,128:]
        else: ra=dotn(jnp.concatenate([w16[i,0],w16[i,1]],1),jnp.concatenate([u,B],0))
        wt=jnp.where(k<cnt,jnp.where(i==j,0.5,1.0),0.0).astype(f32)
        R[i]+=wt*rh
        R[j]+=wt*ra
    for p in range(NB-1): sa(p,p)
    if CARRY:
        def body(t,prev):
            for g in range(G):
                k=t*G+g
                sa(k+NB-1,(g+NB-1)%NB)
                cur=sv(k,g%NB)
                sbc(k-1,prev) if g else sbc(jnp.maximum(k-1,0),prev)
                prev=cur
            return prev
        z=jnp.zeros((128,128),bf)
        prev=lax.fori_loop(0,(cnt+G-1)//G,body,(z,z,z))
        sbc((cnt+G-1)//G*G-1,prev)
    else:
        def body(t,_):
            prev=None
            for g in range(G):
                k=t*G+g
                sa(k+NB-1,(g+NB-1)%NB)
                cur=sv(k,g%NB)
                if g: sbc(k-1,prev)
                prev=cur
            sbc(t*G+G-1,prev)
            return _
        lax.fori_loop(0,(cnt+G-1)//G,body,0)
    def epi(t,_):
        for e in range(8):
            c=t*8+e
            r=R[c]; T=state[c]; rho=T[6:7]
            r0=r[0:1]+r[1:2]+r[2:3]
            for k in range(3):
                rx=r[3+3*k:4+3*k]+r[4+3*k:5+3*k]+r[5+3*k:6+3*k]
                out[c,k:k+1]=(rx-T[k:k+1]*r0)/rho
            out[c,3:4]=r[12:13]+r[13:14]
        return _
    lax.fori_loop(0,ncell//8,epi,0)
PU=4
CARRY=False
def call(G,home,away,cnt,state,NB=2):
    global CARRY
    CARRY='carry' in F
    global PU
    for f in F:
        if f.startswith('pu'): PU=int(f[2:])
    if 'nb4' in F: NB=4
    if 'nb8' in F: NB=8
    nc=state.shape[0]
    return pl.pallas_call(functools.partial(kern,G,NB),
      out_shape=jax.ShapeDtypeStruct((nc,4,128),f32),
      in_specs=[pl.BlockSpec(memory_space=pltpu.SMEM)]*3+[pl.BlockSpec(memory_space=pltpu.VMEM)],
      out_specs=pl.BlockSpec(memory_space=pltpu.VMEM),
      scratch_shapes=[pltpu.VMEM((nc,128,K),bf),pltpu.VMEM((nc,2,K,128),bf),pltpu.VMEM((nc,2,128,128),f32),pltpu.VMEM((nc,8,128),f32),pltpu.VMEM((nc,2,16,128),bf),pltpu.VMEM((nc,16,128),f32),
        pltpu.VMEM((NB,2,128,128),f32)],
      compiler_params=pltpu.CompilerParams(vmem_limit_bytes=60<<20))(home,away,cnt,state)
from jax.sharding import PartitionSpec as PS

GZ = 16
CFL_NUMBER = 0.25
SOUND = 10.0
GROUP = 32


def shift(array, by):
    peers = lax.axis_size("slab")
    return lax.ppermute(array, "slab", [(i, i + by) for i in range(peers) if 0 <= i + by < peers])


def per_device(positions, velocity, density, mass, walls, pairs, counts):
    cells = density.shape[0]
    slots = pairs.shape[1]
    slab = lax.axis_index("slab").astype(jnp.float32)
    middle = jnp.stack([slab + 1.0, jnp.float32(4.0), jnp.float32(8.0)])[:, None, None]
    state = jnp.concatenate([positions - middle, velocity, density[None], mass[None]], 0)
    state = jnp.transpose(state, (1, 0, 2))
    arrived = shift(state, -1)
    one_over = (jnp.arange(8) == 0).astype(jnp.float32)[None, :, None]
    source = jnp.concatenate([state, arrived + one_over], 0)
    speed = jnp.sum(velocity * velocity, axis=0)
    fastest = jnp.max(lax.all_gather(speed, "slab", tiled=True))
    step_size = CFL_NUMBER * SMOOTH / (SOUND + jnp.sqrt(fastest))
    extra = -slots % GROUP
    home = jnp.pad(jnp.minimum(pairs[0], pairs[1]), (0, extra + GROUP))
    away = jnp.pad(jnp.maximum(pairs[0], pairs[1]), (0, extra + GROUP))
    live = jnp.arange(slots) < counts[0]
    inner = jnp.any(live & (jnp.minimum(pairs[0], pairs[1]) >= cells))
    facts = jnp.stack([counts[0], inner.astype(jnp.int32)])
    totals = call(GROUP, home, away, facts, source)
    returned = shift(totals[cells:], 1)
    summed = jnp.transpose(totals[:cells] + returned, (1, 0, 2))
    gravity = jnp.array([0.0, 0.0, -9.81], jnp.float32)[:, None, None]
    fluid = (walls == 0)[None]
    new_velocity = jnp.where(fluid, velocity + step_size * (summed[:3] + gravity), velocity)
    within = jnp.arange(cells, dtype=jnp.int32)
    corner = jnp.stack(
        [
            jnp.zeros((cells,), jnp.float32) + slab,
            (within // GZ).astype(jnp.float32),
            (within % GZ).astype(jnp.float32),
        ]
    )[:, :, None]
    offsets = positions - corner
    new_offsets = jnp.where(fluid, offsets + step_size * new_velocity, offsets)
    new_density = density + step_size * summed[3]
    return (new_offsets, new_velocity, new_density)


def solution(mesh):
    wide = PS(None, ("runs", "slab"), None)
    flat = PS(("runs", "slab"), None)
    return jax.shard_map(
        per_device,
        mesh=mesh,
        in_specs=(wide, wide, flat, flat, flat, PS(None, ("runs", "slab")), PS(("runs", "slab"))),
        out_specs=(wide, wide, flat),
        check_vma=False,
    )
```

```python
import functools
import math

import jax
import jax.numpy as jnp
from jax import lax
from jax.experimental import pallas as pl
from jax.experimental.pallas import tpu as pltpu
from jax.sharding import PartitionSpec as P

GY = 8
GZ = 16
SMOOTH = 0.5
SOUND = 10.0
CFL_NUMBER = 0.25
GRAD_SCALE = -105.0 / (16.0 * math.pi * SMOOTH**5)
ETA = 0.01 * SMOOTH * SMOOTH
TINY = 1e-12
DEPTH = 48
GROUP = 32
AHEAD = 4
BUILD = 8
bf16 = jnp.bfloat16
f32 = jnp.float32


def split3(value):
    first = value.astype(bf16).astype(f32)
    rest = value - first
    second = rest.astype(bf16).astype(f32)
    third = (rest - second).astype(bf16).astype(f32)
    return first, second, third


def tait_pressure(density):
    square = density * density
    return SOUND * SOUND / 7.0 * (square * square * square * density - 1.0)


def dot_rows(left, right):
    return lax.dot_general(left, right, (((1,), (0,)), ((), ())), preferred_element_type=f32)


def dot_lanes(left, right):
    return lax.dot_general(left, right, (((1,), (1,)), ((), ())), preferred_element_type=f32)


def spread(row, count):
    return jnp.broadcast_to(row, (count, row.shape[1]))


def build_cell(cell, local, source, corner_x, as_home, tables):
    home_tab, away_tab, side_tab, row_tab, weight_tab = tables
    row8 = lax.broadcasted_iota(jnp.int32, (8, 128), 0)
    raw = source[:, local, :]
    shift = jnp.where(row8 == 0, corner_x, jnp.where(row8 == 1, 0.5 * GY, jnp.where(row8 == 2, 0.5 * GZ, 0.0)))
    state = raw - shift
    x, y, z, vx, vy, vz, rho, mass = [state[k : k + 1] for k in range(8)]
    square = split3(spread(x * x + y * y + z * z, 8))
    along = split3(spread(x * vx + y * vy + z * vz, 8))
    parts = split3(state)
    swapped = split3(jnp.where(row8 < 3, pltpu.roll(state, 5, 0), pltpu.roll(state, 3, 0)))
    one = jnp.ones((8, 128), f32)
    none = jnp.zeros((8, 128), f32)
    extras = [(one, square[i], -0.5 * along[i]) for i in range(3)]
    extras += [(square[i], one, none) for i in range(3)]
    extras += [(along[i], none, -0.5 * one) for i in range(3)]
    extras += [(none, none, none)] * 3
    home_rows, dist_rows, close_rows = [], [], []
    for group, (p, q) in enumerate([(0, 0), (0, 1), (1, 0), (1, 1), (0, 2), (2, 0)]):
        six, seven = extras[2 * group], extras[2 * group + 1]
        home_rows.append(jnp.where(row8 < 6, parts[p], jnp.where(row8 == 6, six[0], seven[0])))
        dist_rows.append(
            jnp.where(row8 < 3, -2.0 * parts[q], jnp.where(row8 < 6, 0.0, jnp.where(row8 == 6, six[1], seven[1])))
        )
        close_rows.append(jnp.where(row8 < 6, 0.5 * swapped[q], jnp.where(row8 == 6, six[2], seven[2])))
    away_tab[cell, 0] = jnp.concatenate(dist_rows, 0).astype(bf16)
    away_tab[cell, 1] = jnp.concatenate(close_rows, 0).astype(bf16)
    pressure = tait_pressure(rho)
    side = jnp.where(
        row8 == 0,
        spread(20.0 * rho - 20.0, 8),
        jnp.where(row8 == 1, spread(pressure, 8), spread(20.0 * rho + 20.0, 8)),
    )
    row_tab[cell] = side
    if as_home:
        side_parts = split3(jnp.where(row8 < 2, side, 0.0))
        turned = jnp.transpose(jnp.concatenate(home_rows + list(side_parts) + [none], 0)).astype(bf16)
        home_tab[cell] = turned[:, :DEPTH]
        pick = lax.broadcasted_iota(jnp.int32, (80, 256), 0)
        half = lax.broadcasted_iota(jnp.int32, (80, 256), 1) // 128
        select = jnp.where((pick >= DEPTH) & (pick < DEPTH + 24) & (pick % 8 == half), 1.0, 0.0).astype(bf16)
        wide = dot_rows(turned, select)
        side_tab[cell, 0] = wide[:, :128]
        side_tab[cell, 1] = wide[:, 128:]
    volume = GRAD_SCALE * mass / rho
    row16 = lax.broadcasted_iota(jnp.int32, (16, 128), 0)
    base = spread(volume, 16) * jnp.where(
        row16 < 3, 1.0, jnp.where(row16 < 6, spread(x, 16), jnp.where(row16 < 9, spread(y, 16), spread(z, 16)))
    )
    first, second, third = split3(base)
    which = row16 % 3
    push = jnp.where(row16 < 12, jnp.where(which == 0, first, jnp.where(which == 1, second, third)), 0.0)
    first, second, third = split3(spread(volume * (-1.0 / 20.0), 16))
    rate = jnp.where(row16 == 12, first, jnp.where(row16 == 13, second, 0.0))
    weight_tab[cell, 0] = push.astype(bf16)
    weight_tab[cell, 1] = rate.astype(bf16)


def pair_kernel(
    home_ref, away_ref, facts_ref, own, ahead, own_out, ahead_out,
    home_tab, away_tab, side_tab, row_tab, weight_tab, sums, products,
):
    cells = own.shape[1]
    tables = (home_tab, away_tab, side_tab, row_tab, weight_tab)
    corner_x = facts_ref[2].astype(f32) + 1.0

    def build(source, offset, as_home):
        def step(at, carry):
            for inner in range(BUILD):
                local = at * BUILD + inner
                build_cell(offset + local, local, source, corner_x, as_home, tables)
            return carry

        lax.fori_loop(0, cells // BUILD, step, 0)

    sums[...] = jnp.zeros_like(sums)
    build(own, 0, True)
    ahead_homes = facts_ref[1] > 0

    @pl.when(ahead_homes)
    def _():
        build(ahead, cells, True)

    @pl.when(jnp.logical_not(ahead_homes))
    def _():
        build(ahead, cells, False)

    count = facts_ref[0]

    def form(k, slot):
        j = away_ref[k]
        both = dot_rows(home_tab[home_ref[k]], jnp.concatenate([away_tab[j, 0], away_tab[j, 1]], 1))
        products[slot, 0] = both[:, :128]
        products[slot, 1] = both[:, 128:]

    def factors(k, slot):
        i = home_ref[k]
        j = away_ref[k]
        dist_sq = jnp.maximum(products[slot, 0], TINY)
        closing = products[slot, 1]
        density_b, pressure_b, raised_b = row_tab[j, 0:1], row_tab[j, 1:2], row_tab[j, 2:3]
        density_a = side_tab[i, 0]
        shell = jnp.maximum(1.0 - dist_sq * lax.rsqrt(dist_sq), 0.0)
        cube = shell * shell * shell
        approach = closing * (density_a + raised_b)
        push = (cube * ((side_tab[i, 1] + pressure_b) + jnp.maximum(approach, 0.0))).astype(bf16)
        dist_n, cube_n = dist_sq.astype(bf16), cube.astype(bf16)
        approach_n, closing_n = approach.astype(bf16), closing.astype(bf16)
        shape = dist_n / (dist_n + bf16(ETA))
        skew = (density_b.astype(bf16) - density_a.astype(bf16)) * (shape + closing_n)
        return push, cube_n * (approach_n - skew), cube_n * (approach_n + skew)

    def gather(k, values):
        push, rate_home, rate_away = values
        i = home_ref[k]
        j = away_ref[k]
        to_home = dot_lanes(
            jnp.concatenate([weight_tab[j, 0], weight_tab[j, 1]], 1), jnp.concatenate([push, rate_home], 1)
        )
        to_away = dot_rows(
            jnp.concatenate([weight_tab[i, 0], weight_tab[i, 1]], 1), jnp.concatenate([push, rate_away], 0)
        )
        spare = 2 * cells
        sums[jnp.where(k < count, i, spare)] += to_home
        sums[jnp.where((k < count) & (i != j), j, spare)] += to_away

    for k in range(AHEAD - 1):
        form(k, k)

    def turn(at, carry):
        held = None
        for inner in range(GROUP):
            k = at * GROUP + inner
            form(k + AHEAD - 1, (inner + AHEAD - 1) % AHEAD)
            values = factors(k, inner % AHEAD)
            if inner:
                gather(k - 1, held)
            held = values
        gather(at * GROUP + GROUP - 1, held)
        return carry

    lax.fori_loop(0, (count + GROUP - 1) // GROUP, turn, 0)

    def finish(source, offset, out):
        def step(at, carry):
            for inner in range(BUILD):
                local = at * BUILD + inner
                total = sums[offset + local]
                middle = (corner_x, 0.5 * GY, 0.5 * GZ)
                rho = source[6, pl.ds(local, 1), :]
                plain = total[0:1] + total[1:2] + total[2:3]
                for k in range(3):
                    moment = total[3 + 3 * k : 4 + 3 * k] + total[4 + 3 * k : 5 + 3 * k] + total[5 + 3 * k : 6 + 3 * k]
                    place = source[k, pl.ds(local, 1), :] - middle[k]
                    out[k, pl.ds(local, 1), :] = (moment - place * plain) / rho
                out[3, pl.ds(local, 1), :] = total[12:13] + total[13:14]
            return carry

        lax.fori_loop(0, cells // BUILD, step, 0)

    finish(ahead, cells, ahead_out)
    finish(own, 0, own_out)


def pair_sums(home, away, facts, own, ahead):
    cells = own.shape[1]
    shape = jax.ShapeDtypeStruct((4, cells, 128), f32)
    both = 2 * cells
    return pl.pallas_call(
        pair_kernel,
        out_shape=(shape, shape),
        in_specs=[pl.BlockSpec(memory_space=pltpu.SMEM)] * 3 + [pl.BlockSpec(memory_space=pltpu.VMEM)] * 2,
        out_specs=[pl.BlockSpec(memory_space=pltpu.VMEM)] * 2,
        scratch_shapes=[
            pltpu.VMEM((both, 128, DEPTH), bf16),
            pltpu.VMEM((both, 2, DEPTH, 128), bf16),
            pltpu.VMEM((both, 2, 128, 128), f32),
            pltpu.VMEM((both, 8, 128), f32),
            pltpu.VMEM((both, 2, 16, 128), bf16),
            pltpu.VMEM((both + 1, 16, 128), f32),
            pltpu.VMEM((AHEAD, 2, 128, 128), f32),
        ],
        compiler_params=pltpu.CompilerParams(vmem_limit_bytes=58 << 20),
        cost_estimate=pl.CostEstimate(flops=4 * 10**9, transcendentals=5 * 10**7, bytes_accessed=2 * 10**6),
    )(home, away, facts, own, ahead)


def shift(array, by):
    peers = lax.axis_size("slab")
    return lax.ppermute(array, "slab", [(i, i + by) for i in range(peers) if 0 <= i + by < peers])


def largest(value):
    peers = lax.axis_size("slab")
    step = 1
    while step < peers:
        moved = lax.ppermute(value, "slab", [(i, (i + step) % peers) for i in range(peers)])
        value = jnp.maximum(value, moved)
        step *= 2
    return jnp.max(value)


def per_device(positions, velocity, density, mass, walls, pairs, counts):
    cells = density.shape[0]
    slots = pairs.shape[1]
    slab = lax.axis_index("slab")
    state = jnp.concatenate([positions, velocity, density[None], mass[None]], 0)
    arrived = shift(state, -1)
    speed = jnp.max(jnp.sum(velocity * velocity, axis=0).reshape(-1, 8, 128), axis=0)
    fastest = largest(speed)
    step_size = CFL_NUMBER * SMOOTH / (SOUND + jnp.sqrt(fastest))
    low = jnp.minimum(pairs[0], pairs[1])
    high = jnp.maximum(pairs[0], pairs[1])
    live = jnp.arange(slots) < counts[0]
    inner = jnp.any(live & (low >= cells))
    facts = jnp.stack([counts[0], inner.astype(jnp.int32), slab.astype(jnp.int32)])
    extra = -slots % GROUP + AHEAD
    home = jnp.pad(low, (0, extra))
    away = jnp.pad(high, (0, extra))
    kept, lent = pair_sums(home, away, facts, state, arrived)
    summed = kept + shift(lent, 1)
    gravity = jnp.array([0.0, 0.0, -9.81], f32)[:, None, None]
    fluid = (walls == 0)[None]
    new_velocity = jnp.where(fluid, velocity + step_size * (summed[:3] + gravity), velocity)
    within = jnp.arange(cells, dtype=jnp.int32)
    corner = jnp.stack(
        [
            jnp.zeros((cells,), f32) + slab.astype(f32),
            (within // GZ).astype(f32),
            (within % GZ).astype(f32),
        ]
    )[:, :, None]
    offsets = positions - corner
    new_offsets = jnp.where(fluid, offsets + step_size * new_velocity, offsets)
    new_density = density + step_size * summed[3]
    return (new_offsets, new_velocity, new_density)


def solution(mesh):
    wide = P(None, ("runs", "slab"), None)
    flat = P(("runs", "slab"), None)
    return jax.shard_map(
        per_device,
        mesh=mesh,
        in_specs=(wide, wide, flat, flat, flat, P(None, ("runs", "slab")), P(("runs", "slab"))),
        out_specs=(wide, wide, flat),
        check_vma=False,
    )
```

```python
import functools
import math

import jax
import jax.numpy as jnp
from jax import lax
from jax.experimental import pallas as pl
from jax.experimental.pallas import tpu as pltpu
from jax.sharding import PartitionSpec as P

GY = 8
GZ = 16
SMOOTH = 0.5
SOUND = 10.0
CFL_NUMBER = 0.25
GRAD_SCALE = -105.0 / (16.0 * math.pi * SMOOTH**5)
ETA = 0.01 * SMOOTH * SMOOTH
TINY = 1e-12
DEPTH = 48
GROUP = 32
AHEAD = 4
BUILD = 8
bf16 = jnp.bfloat16
f32 = jnp.float32


def split3(value):
    first = value.astype(bf16).astype(f32)
    rest = value - first
    second = rest.astype(bf16).astype(f32)
    third = (rest - second).astype(bf16).astype(f32)
    return first, second, third


def tait_pressure(density):
    square = density * density
    return SOUND * SOUND / 7.0 * (square * square * square * density - 1.0)


def dot_rows(left, right):
    return lax.dot_general(left, right, (((1,), (0,)), ((), ())), preferred_element_type=f32)


def dot_lanes(left, right):
    return lax.dot_general(left, right, (((1,), (1,)), ((), ())), preferred_element_type=f32)


def spread(row, count):
    return jnp.broadcast_to(row, (count, row.shape[1]))


def rows_of(values):
    row = lax.broadcasted_iota(jnp.int32, (8, 128), 0)
    out = jnp.zeros((8, 128), f32)
    for at, value in enumerate(values):
        if value:
            out = jnp.where(row == at, value, out)
    return out


def centred(source, local, corner_x):
    row = lax.broadcasted_iota(jnp.int32, (8, 128), 0)
    middle = jnp.where(row == 0, corner_x, jnp.where(row == 1, 0.5 * GY, jnp.where(row == 2, 0.5 * GZ, 0.0)))
    return source[:, local, :] - middle


def build_cell(cell, local, source, corner_x, as_home, tables):
    home_tab, away_tab, side_tab, row_tab, weight_tab = tables
    row = lax.broadcasted_iota(jnp.int32, (8, 128), 0)
    state = centred(source, local, corner_x)
    x, y, z, vx, vy, vz, rho, mass = [state[k : k + 1] for k in range(8)]
    square = spread(x * x + y * y + z * z, 8)
    along = spread(x * vx + y * vy + z * vz, 8)
    full = jnp.where(row < 6, state, jnp.where(row == 6, square, along))
    parts = split3(full)
    turned = jnp.where(row < 3, pltpu.roll(state, 5, 0), jnp.where(row < 6, pltpu.roll(state, 3, 0), along))
    swapped = split3(turned * rows_of([0.5] * 6 + [-0.5]))
    scale = rows_of([-2.0] * 3 + [0.0] * 3 + [1.0])
    scale_low = rows_of([-2.0] * 3)
    unit = rows_of([0.0] * 6 + [1.0])
    minus = rows_of([0.0] * 7 + [-0.5])
    own_terms = [(0, 0), (1, 1), (2, 0)]
    plain_terms = [(0, 1), (0, 2), (1, 0)]
    held = [jnp.where(row < 6, parts[p], unit) for p in range(2)]
    home_rows = [parts[p] for p, _ in own_terms] + [held[p] for p, _ in plain_terms]
    dist_rows = [parts[q] * scale_low + unit for _, q in own_terms] + [parts[q] * scale for _, q in plain_terms]
    close_rows = [jnp.where(row < 6, swapped[q], minus) for _, q in own_terms] + [swapped[q] for _, q in plain_terms]
    away_tab[cell, 0] = jnp.concatenate(dist_rows, 0).astype(bf16)
    away_tab[cell, 1] = jnp.concatenate(close_rows, 0).astype(bf16)
    dense = spread(20.0 * rho, 8)
    side = jnp.where(row == 0, dense - 20.0, jnp.where(row == 1, spread(tait_pressure(rho), 8), dense + 20.0))
    row_tab[cell] = side
    if as_home:
        side_parts = split3(side)
        columns = jnp.transpose(jnp.concatenate(home_rows + list(side_parts) + [side_parts[0]], 0)).astype(bf16)
        home_tab[cell] = columns[:, :DEPTH]
        pick = lax.broadcasted_iota(jnp.int32, (DEPTH + 32, 256), 0)
        half = lax.broadcasted_iota(jnp.int32, (DEPTH + 32, 256), 1) // 128
        chosen = (pick >= DEPTH) & (pick < DEPTH + 24) & (pick % 8 == half)
        wide = dot_rows(columns, jnp.where(chosen, 1.0, 0.0).astype(bf16))
        side_tab[cell, 0] = wide[:, :128]
        side_tab[cell, 1] = wide[:, 128:]
    volume = spread(GRAD_SCALE * mass / rho, 8)
    factor = jnp.where(row == 0, 1.0, jnp.where(row == 4, -1.0 / 20.0, pltpu.roll(state, 1, 0)))
    first, second, third = split3(volume * factor)
    none = jnp.zeros((8, 128), f32)
    push_low = jnp.where(row < 4, first, pltpu.roll(third, 4, 0))
    push_high = jnp.where(row < 4, second, 0.0)
    rate_high = jnp.where(row == 4, first, jnp.where(row == 5, pltpu.roll(second, 1, 0), 0.0))
    weight_tab[cell, 0] = jnp.concatenate([push_low, push_high], 0).astype(bf16)
    weight_tab[cell, 1] = jnp.concatenate([none, rate_high], 0).astype(bf16)


def pair_kernel(
    home_ref, away_ref, facts_ref, own, ahead, own_out, ahead_out,
    home_tab, away_tab, side_tab, row_tab, weight_tab, sums, products,
):
    cells = own.shape[1]
    tables = (home_tab, away_tab, side_tab, row_tab, weight_tab)
    corner_x = facts_ref[2].astype(f32) + 1.0

    def build(source, offset, as_home):
        def step(at, carry):
            for inner in range(BUILD):
                local = at * BUILD + inner
                build_cell(offset + local, local, source, corner_x, as_home, tables)
            return carry

        lax.fori_loop(0, cells // BUILD, step, 0)

    sums[...] = jnp.zeros_like(sums)
    build(own, 0, True)
    ahead_homes = facts_ref[1] > 0

    @pl.when(ahead_homes)
    def _():
        build(ahead, cells, True)

    @pl.when(jnp.logical_not(ahead_homes))
    def _():
        build(ahead, cells, False)

    count = facts_ref[0]

    def form(k, slot):
        j = away_ref[k]
        both = dot_rows(home_tab[home_ref[k]], jnp.concatenate([away_tab[j, 0], away_tab[j, 1]], 1))
        products[slot, 0] = both[:, :128]
        products[slot, 1] = both[:, 128:]

    def factors(k, slot):
        i = home_ref[k]
        j = away_ref[k]
        dist_sq = jnp.maximum(products[slot, 0], TINY)
        closing = products[slot, 1]
        density_b, pressure_b, raised_b = row_tab[j, 0:1], row_tab[j, 1:2], row_tab[j, 2:3]
        density_a = side_tab[i, 0]
        shell = jnp.maximum(1.0 - dist_sq * lax.rsqrt(dist_sq), 0.0)
        cube = shell * shell * shell
        approach = closing * (density_a + raised_b)
        push = (cube * ((side_tab[i, 1] + pressure_b) + jnp.maximum(approach, 0.0))).astype(bf16)
        dist_n, cube_n = dist_sq.astype(bf16), cube.astype(bf16)
        approach_n, closing_n = approach.astype(bf16), closing.astype(bf16)
        shape = dist_n / (dist_n + bf16(ETA))
        skew = (density_b.astype(bf16) - density_a.astype(bf16)) * (shape + closing_n)
        return push, cube_n * (approach_n - skew), cube_n * (approach_n + skew)

    def gather(k, values):
        push, rate_home, rate_away = values
        i = home_ref[k]
        j = away_ref[k]
        to_home = dot_lanes(
            jnp.concatenate([weight_tab[j, 0], weight_tab[j, 1]], 1), jnp.concatenate([push, rate_home], 1)
        )
        to_away = dot_rows(
            jnp.concatenate([weight_tab[i, 0], weight_tab[i, 1]], 1), jnp.concatenate([push, rate_away], 0)
        )
        spare = 2 * cells
        sums[jnp.where(k < count, i, spare)] += to_home
        sums[jnp.where((k < count) & (i != j), j, spare)] += to_away

    for k in range(AHEAD - 1):
        form(k, k)

    def turn(at, carry):
        held = None
        for inner in range(GROUP):
            k = at * GROUP + inner
            form(k + AHEAD - 1, (inner + AHEAD - 1) % AHEAD)
            values = factors(k, inner % AHEAD)
            if inner:
                gather(k - 1, held)
            held = values
        gather(at * GROUP + GROUP - 1, held)
        return carry

    lax.fori_loop(0, (count + GROUP - 1) // GROUP, turn, 0)

    def finish(source, offset, out):
        def step(at, carry):
            for inner in range(BUILD):
                local = at * BUILD + inner
                low, high = sums[offset + local, 0:8], sums[offset + local, 8:16]
                state = centred(source, local, corner_x)
                total = low + pltpu.roll(low, 4, 0) + high
                force = (total - pltpu.roll(state, 1, 0) * spread(total[0:1], 8)) / spread(state[6:7], 8)
                for k in range(3):
                    out[k, pl.ds(local, 1), :] = force[k + 1 : k + 2]
                out[3, pl.ds(local, 1), :] = high[4:5] + high[5:6]
            return carry

        lax.fori_loop(0, cells // BUILD, step, 0)

    finish(ahead, cells, ahead_out)
    finish(own, 0, own_out)


def pair_sums(home, away, facts, own, ahead):
    cells = own.shape[1]
    shape = jax.ShapeDtypeStruct((4, cells, 128), f32)
    both = 2 * cells
    return pl.pallas_call(
        pair_kernel,
        out_shape=(shape, shape),
        in_specs=[pl.BlockSpec(memory_space=pltpu.SMEM)] * 3 + [pl.BlockSpec(memory_space=pltpu.VMEM)] * 2,
        out_specs=[pl.BlockSpec(memory_space=pltpu.VMEM)] * 2,
        scratch_shapes=[
            pltpu.VMEM((both, 128, DEPTH), bf16),
            pltpu.VMEM((both, 2, DEPTH, 128), bf16),
            pltpu.VMEM((both, 2, 128, 128), f32),
            pltpu.VMEM((both, 8, 128), f32),
            pltpu.VMEM((both, 2, 16, 128), bf16),
            pltpu.VMEM((both + 1, 16, 128), f32),
            pltpu.VMEM((AHEAD, 2, 128, 128), f32),
        ],
        compiler_params=pltpu.CompilerParams(vmem_limit_bytes=58 << 20),
        cost_estimate=pl.CostEstimate(flops=4 * 10**9, transcendentals=5 * 10**7, bytes_accessed=2 * 10**6),
    )(home, away, facts, own, ahead)


def shift(array, by):
    peers = lax.axis_size("slab")
    return lax.ppermute(array, "slab", [(i, i + by) for i in range(peers) if 0 <= i + by < peers])


def pass_on(value, step):
    peers = lax.axis_size("slab")
    moved = lax.ppermute(value, "slab", [(i, (i + step) % peers) for i in range(peers)])
    return jnp.maximum(value, moved)


def per_device(positions, velocity, density, mass, walls, pairs, counts):
    cells = density.shape[0]
    slots = pairs.shape[1]
    slab = lax.axis_index("slab")
    state = jnp.concatenate([positions, velocity, density[None], mass[None]], 0)
    arrived = shift(state, -1)
    speed = jnp.max(jnp.sum(velocity * velocity, axis=0).reshape(-1, 8, 128), axis=0)
    reach = 1
    while 2 * reach < lax.axis_size("slab"):
        speed = pass_on(speed, reach)
        reach *= 2
    low = jnp.minimum(pairs[0], pairs[1])
    high = jnp.maximum(pairs[0], pairs[1])
    live = jnp.arange(slots) < counts[0]
    inner = jnp.any(live & (low >= cells))
    facts = jnp.stack([counts[0], inner.astype(jnp.int32), slab.astype(jnp.int32)])
    extra = -slots % GROUP + AHEAD
    home = jnp.pad(low, (0, extra))
    away = jnp.pad(high, (0, extra))
    kept, lent = pair_sums(home, away, facts, state, arrived)
    returned = shift(lent, 1)
    speed, _ = lax.optimization_barrier((speed, lent))
    fastest = jnp.max(pass_on(speed, reach))
    step_size = CFL_NUMBER * SMOOTH / (SOUND + jnp.sqrt(fastest))
    gravity = jnp.array([0.0, 0.0, -9.81], f32)[:, None, None]
    fluid = (walls == 0)[None]
    new_velocity = jnp.where(fluid, velocity + step_size * (kept[:3] + returned[:3] + gravity), velocity)
    within = jnp.arange(cells, dtype=jnp.int32)
    corner = jnp.stack(
        [
            jnp.zeros((cells,), f32) + slab.astype(f32),
            (within // GZ).astype(f32),
            (within % GZ).astype(f32),
        ]
    )[:, :, None]
    offsets = positions - corner
    new_offsets = jnp.where(fluid, offsets + step_size * new_velocity, offsets)
    new_density = density + step_size * (kept[3] + returned[3])
    return (new_offsets, new_velocity, new_density)


def solution(mesh):
    wide = P(None, ("runs", "slab"), None)
    flat = P(("runs", "slab"), None)
    return jax.shard_map(
        per_device,
        mesh=mesh,
        in_specs=(wide, wide, flat, flat, flat, P(None, ("runs", "slab")), P(("runs", "slab"))),
        out_specs=(wide, wide, flat),
        check_vma=False,
    )
```

```python
import functools
import math

import jax
import jax.numpy as jnp
from jax import lax
from jax.experimental import pallas as pl
from jax.experimental.pallas import tpu as pltpu
from jax.sharding import PartitionSpec as P

GY = 8
GZ = 16
SMOOTH = 0.5
SOUND = 10.0
CFL_NUMBER = 0.25
GRAD_SCALE = -105.0 / (16.0 * math.pi * SMOOTH**5)
ETA = 0.01 * SMOOTH * SMOOTH
TINY = 1e-12
DEPTH = 48
GROUP = 32
AHEAD = 4
BUILD = 8
bf16 = jnp.bfloat16
f32 = jnp.float32


def split3(value):
    first = value.astype(bf16).astype(f32)
    rest = value - first
    second = rest.astype(bf16).astype(f32)
    third = (rest - second).astype(bf16).astype(f32)
    return first, second, third


def tait_pressure(density):
    square = density * density
    return SOUND * SOUND / 7.0 * (square * square * square * density - 1.0)


def dot_rows(left, right):
    return lax.dot_general(left, right, (((1,), (0,)), ((), ())), preferred_element_type=f32)


def dot_lanes(left, right):
    return lax.dot_general(left, right, (((1,), (1,)), ((), ())), preferred_element_type=f32)


def spread(row, count):
    return jnp.broadcast_to(row, (count, row.shape[1]))


def rows_of(values):
    row = lax.broadcasted_iota(jnp.int32, (8, 128), 0)
    out = jnp.zeros((8, 128), f32)
    for at, value in enumerate(values):
        if value:
            out = jnp.where(row == at, value, out)
    return out


def centred(source, local, corner_x):
    row = lax.broadcasted_iota(jnp.int32, (8, 128), 0)
    middle = jnp.where(row == 0, corner_x, jnp.where(row == 1, 0.5 * GY, jnp.where(row == 2, 0.5 * GZ, 0.0)))
    return source[:, local, :] - middle


def build_cell(cell, local, source, corner_x, as_home, tables):
    home_tab, away_tab, side_tab, row_tab, weight_tab = tables
    row = lax.broadcasted_iota(jnp.int32, (8, 128), 0)
    state = centred(source, local, corner_x)
    x, y, z, vx, vy, vz, rho, mass = [state[k : k + 1] for k in range(8)]
    square = spread(x * x + y * y + z * z, 8)
    along = spread(x * vx + y * vy + z * vz, 8)
    full = jnp.where(row < 6, state, jnp.where(row == 6, square, along))
    parts = split3(full)
    turned = jnp.where(row < 3, pltpu.roll(state, 5, 0), jnp.where(row < 6, pltpu.roll(state, 3, 0), along))
    swapped = split3(turned * rows_of([0.5] * 6 + [-0.5]))
    scale = rows_of([-2.0] * 3 + [0.0] * 3 + [1.0])
    scale_low = rows_of([-2.0] * 3)
    unit = rows_of([0.0] * 6 + [1.0])
    minus = rows_of([0.0] * 7 + [-0.5])
    own_terms = [(0, 0), (1, 1), (2, 0)]
    plain_terms = [(0, 1), (0, 2), (1, 0)]
    held = [jnp.where(row < 6, parts[p], unit) for p in range(2)]
    home_rows = [parts[p] for p, _ in own_terms] + [held[p] for p, _ in plain_terms]
    dist_rows = [parts[q] * scale_low + unit for _, q in own_terms] + [parts[q] * scale for _, q in plain_terms]
    close_rows = [jnp.where(row < 6, swapped[q], minus) for _, q in own_terms] + [swapped[q] for _, q in plain_terms]
    away_tab[cell, 0] = jnp.concatenate(dist_rows, 0).astype(bf16)
    away_tab[cell, 1] = jnp.concatenate(close_rows, 0).astype(bf16)
    dense = spread(20.0 * rho, 8)
    side = jnp.where(row == 0, dense - 20.0, jnp.where(row == 1, spread(tait_pressure(rho), 8), dense + 20.0))
    row_tab[cell] = side
    if as_home:
        side_parts = split3(side)
        columns = jnp.transpose(jnp.concatenate(home_rows + list(side_parts) + [side_parts[0]], 0)).astype(bf16)
        home_tab[cell] = columns[:, :DEPTH]
        pick = lax.broadcasted_iota(jnp.int32, (DEPTH + 32, 256), 0)
        half = lax.broadcasted_iota(jnp.int32, (DEPTH + 32, 256), 1) // 128
        chosen = (pick >= DEPTH) & (pick < DEPTH + 24) & (pick % 8 == half)
        wide = dot_rows(columns, jnp.where(chosen, 1.0, 0.0).astype(bf16))
        side_tab[cell, 0] = wide[:, :128]
        side_tab[cell, 1] = wide[:, 128:]
    volume = spread(GRAD_SCALE * mass / rho, 8)
    factor = jnp.where(row == 0, 1.0, jnp.where(row == 4, -1.0 / 20.0, pltpu.roll(state, 1, 0)))
    first, second, third = split3(volume * factor)
    none = jnp.zeros((8, 128), f32)
    push_low = jnp.where(row < 4, first, pltpu.roll(third, 4, 0))
    push_high = jnp.where(row < 4, second, 0.0)
    rate_high = jnp.where(row == 4, first, jnp.where(row == 5, pltpu.roll(second, 1, 0), 0.0))
    weight_tab[cell, 0] = jnp.concatenate([push_low, push_high], 0).astype(bf16)
    weight_tab[cell, 1] = jnp.concatenate([none, rate_high], 0).astype(bf16)


def pair_kernel(
    pairs_ref, count_ref, slab_ref, pairs_vec, own, ahead, own_out, ahead_out,
    home_tab, away_tab, side_tab, row_tab, weight_tab, sums, products,
):
    cells = own.shape[1]
    slots = pairs_ref.shape[1]
    tables = (home_tab, away_tab, side_tab, row_tab, weight_tab)
    corner_x = slab_ref[0].astype(f32) + 1.0
    count = count_ref[0]

    def home_of(k):
        at = jnp.minimum(k, slots - 1)
        return jnp.minimum(pairs_ref[0, at], pairs_ref[1, at])

    def away_of(k):
        at = jnp.minimum(k, slots - 1)
        return jnp.maximum(pairs_ref[0, at], pairs_ref[1, at])

    def build(source, offset, as_home):
        def step(at, carry):
            for inner in range(BUILD):
                local = at * BUILD + inner
                build_cell(offset + local, local, source, corner_x, as_home, tables)
            return carry

        lax.fori_loop(0, cells // BUILD, step, 0)

    sums[...] = jnp.zeros_like(sums)
    listed = lax.broadcasted_iota(jnp.int32, (1, slots), 1) < count
    lowest = jnp.minimum(pairs_vec[0:1, :], pairs_vec[1:2, :])
    ahead_homes = jnp.max(jnp.where(listed, lowest, 0)) >= cells
    build(own, 0, True)

    @pl.when(ahead_homes)
    def _():
        build(ahead, cells, True)

    @pl.when(jnp.logical_not(ahead_homes))
    def _():
        build(ahead, cells, False)

    def form(k, slot):
        j = away_of(k)
        both = dot_rows(home_tab[home_of(k)], jnp.concatenate([away_tab[j, 0], away_tab[j, 1]], 1))
        products[slot, 0] = both[:, :128]
        products[slot, 1] = both[:, 128:]

    def factors(k, slot):
        i = home_of(k)
        j = away_of(k)
        dist_sq = jnp.maximum(products[slot, 0], TINY)
        closing = products[slot, 1]
        density_b, pressure_b, raised_b = row_tab[j, 0:1], row_tab[j, 1:2], row_tab[j, 2:3]
        density_a = side_tab[i, 0]
        shell = jnp.maximum(1.0 - dist_sq * lax.rsqrt(dist_sq), 0.0)
        cube = shell * shell * shell
        approach = closing * (density_a + raised_b)
        push = (cube * ((side_tab[i, 1] + pressure_b) + jnp.maximum(approach, 0.0))).astype(bf16)
        dist_n, cube_n = dist_sq.astype(bf16), cube.astype(bf16)
        approach_n, closing_n = approach.astype(bf16), closing.astype(bf16)
        shape = dist_n / (dist_n + bf16(ETA))
        skew = (density_b.astype(bf16) - density_a.astype(bf16)) * (shape + closing_n)
        return push, cube_n * (approach_n - skew), cube_n * (approach_n + skew)

    def gather(k, values):
        push, rate_home, rate_away = values
        i = home_of(k)
        j = away_of(k)
        to_home = dot_lanes(
            jnp.concatenate([weight_tab[j, 0], weight_tab[j, 1]], 1), jnp.concatenate([push, rate_home], 1)
        )
        to_away = dot_rows(
            jnp.concatenate([weight_tab[i, 0], weight_tab[i, 1]], 1), jnp.concatenate([push, rate_away], 0)
        )
        spare = 2 * cells
        sums[jnp.where(k < count, i, spare)] += to_home
        sums[jnp.where((k < count) & (i != j), j, spare)] += to_away

    for k in range(AHEAD - 1):
        form(k, k)

    def turn(at, carry):
        held = None
        for inner in range(GROUP):
            k = at * GROUP + inner
            form(k + AHEAD - 1, (inner + AHEAD - 1) % AHEAD)
            values = factors(k, inner % AHEAD)
            if inner:
                gather(k - 1, held)
            held = values
        gather(at * GROUP + GROUP - 1, held)
        return carry

    lax.fori_loop(0, (count + GROUP - 1) // GROUP, turn, 0)

    def finish(source, offset, out):
        def step(at, carry):
            for inner in range(BUILD):
                local = at * BUILD + inner
                low, high = sums[offset + local, 0:8], sums[offset + local, 8:16]
                state = centred(source, local, corner_x)
                total = low + pltpu.roll(low, 4, 0) + high
                force = (total - pltpu.roll(state, 1, 0) * spread(total[0:1], 8)) / spread(state[6:7], 8)
                for k in range(3):
                    out[k, pl.ds(local, 1), :] = force[k + 1 : k + 2]
                out[3, pl.ds(local, 1), :] = high[4:5] + high[5:6]
            return carry

        lax.fori_loop(0, cells // BUILD, step, 0)

    finish(ahead, cells, ahead_out)
    finish(own, 0, own_out)


def pair_sums(pairs, counts, slab, own, ahead):
    cells = own.shape[1]
    shape = jax.ShapeDtypeStruct((4, cells, 128), f32)
    both = 2 * cells
    return pl.pallas_call(
        pair_kernel,
        out_shape=(shape, shape),
        in_specs=[pl.BlockSpec(memory_space=pltpu.SMEM)] * 3
        + [pl.BlockSpec(memory_space=pltpu.VMEM)]
        + [pl.BlockSpec(memory_space=pltpu.VMEM)] * 2,
        out_specs=[pl.BlockSpec(memory_space=pltpu.VMEM)] * 2,
        scratch_shapes=[
            pltpu.VMEM((both, 128, DEPTH), bf16),
            pltpu.VMEM((both, 2, DEPTH, 128), bf16),
            pltpu.VMEM((both, 2, 128, 128), f32),
            pltpu.VMEM((both, 8, 128), f32),
            pltpu.VMEM((both, 2, 16, 128), bf16),
            pltpu.VMEM((both + 1, 16, 128), f32),
            pltpu.VMEM((AHEAD, 2, 128, 128), f32),
        ],
        compiler_params=pltpu.CompilerParams(vmem_limit_bytes=58 << 20),
        cost_estimate=pl.CostEstimate(flops=4 * 10**9, transcendentals=5 * 10**7, bytes_accessed=2 * 10**6),
    )(pairs, counts, slab, pairs, own, ahead)


def shift(array, by):
    peers = lax.axis_size("slab")
    return lax.ppermute(array, "slab", [(i, i + by) for i in range(peers) if 0 <= i + by < peers])


def pass_on(value, step):
    peers = lax.axis_size("slab")
    moved = lax.ppermute(value, "slab", [(i, (i + step) % peers) for i in range(peers)])
    return jnp.maximum(value, moved)


def per_device(positions, velocity, density, mass, walls, pairs, counts):
    cells = density.shape[0]
    slab = lax.axis_index("slab")
    state = jnp.concatenate([positions, velocity, density[None], mass[None]], 0)
    arrived = shift(state, -1)
    speed = jnp.max(jnp.sum(velocity * velocity, axis=0).reshape(-1, 8, 128), axis=0)
    reach = 1
    while 2 * reach < lax.axis_size("slab"):
        speed = pass_on(speed, reach)
        reach *= 2
    kept, lent = pair_sums(pairs, counts, slab.astype(jnp.int32).reshape(1), state, arrived)
    summed = kept + shift(lent, 1)
    speed, _ = lax.optimization_barrier((speed, lent))
    fastest = jnp.max(pass_on(speed, reach))
    step_size = CFL_NUMBER * SMOOTH / (SOUND + jnp.sqrt(fastest))
    gravity = jnp.array([0.0, 0.0, -9.81], f32)[:, None, None]
    fluid = (walls == 0)[None]
    new_velocity = jnp.where(fluid, velocity + step_size * (summed[:3] + gravity), velocity)
    within = jnp.arange(cells, dtype=jnp.int32)
    corner = jnp.stack(
        [
            jnp.zeros((cells,), f32) + slab.astype(f32),
            (within // GZ).astype(f32),
            (within % GZ).astype(f32),
        ]
    )[:, :, None]
    offsets = positions - corner
    new_offsets = jnp.where(fluid, offsets + step_size * new_velocity, offsets)
    new_density = density + step_size * summed[3]
    return (new_offsets, new_velocity, new_density)


def solution(mesh):
    wide = P(None, ("runs", "slab"), None)
    flat = P(("runs", "slab"), None)
    return jax.shard_map(
        per_device,
        mesh=mesh,
        in_specs=(wide, wide, flat, flat, flat, P(None, ("runs", "slab")), P(("runs", "slab"))),
        out_specs=(wide, wide, flat),
        check_vma=False,
    )
```

```python
import functools
import math

import jax
import jax.numpy as jnp
from jax import lax
from jax.experimental import pallas as pl
from jax.experimental.pallas import tpu as pltpu
from jax.sharding import PartitionSpec as P

GY = 8
GZ = 16
SMOOTH = 0.5
SOUND = 10.0
CFL_NUMBER = 0.25
GRAD_SCALE = -105.0 / (16.0 * math.pi * SMOOTH**5)
ETA = 0.01 * SMOOTH * SMOOTH
TINY = 1e-12
DEPTH = 48
GROUP = 32
AHEAD = 4
BUILD = 8
WAYS = 4
bf16 = jnp.bfloat16
f32 = jnp.float32


def split3(value):
    first = value.astype(bf16).astype(f32)
    rest = value - first
    second = rest.astype(bf16).astype(f32)
    third = (rest - second).astype(bf16).astype(f32)
    return first, second, third


def tait_pressure(density):
    square = density * density
    return SOUND * SOUND / 7.0 * (square * square * square * density - 1.0)


def dot_rows(left, right):
    return lax.dot_general(left, right, (((1,), (0,)), ((), ())), preferred_element_type=f32)


def dot_lanes(left, right):
    return lax.dot_general(left, right, (((1,), (1,)), ((), ())), preferred_element_type=f32)


def spread(row, count):
    return jnp.broadcast_to(row, (count, row.shape[1]))


def rows_of(values):
    row = lax.broadcasted_iota(jnp.int32, (8, 128), 0)
    out = jnp.zeros((8, 128), f32)
    for at, value in enumerate(values):
        if value:
            out = jnp.where(row == at, value, out)
    return out


def centred(source, local, corner_x):
    row = lax.broadcasted_iota(jnp.int32, (8, 128), 0)
    middle = jnp.where(row == 0, corner_x, jnp.where(row == 1, 0.5 * GY, jnp.where(row == 2, 0.5 * GZ, 0.0)))
    return source[:, local, :] - middle


def build_cell(cell, local, source, corner_x, as_home, tables):
    home_tab, away_tab, side_tab, row_tab, weight_tab = tables
    row = lax.broadcasted_iota(jnp.int32, (8, 128), 0)
    state = centred(source, local, corner_x)
    x, y, z, vx, vy, vz, rho, mass = [state[k : k + 1] for k in range(8)]
    square = spread(x * x + y * y + z * z, 8)
    along = spread(x * vx + y * vy + z * vz, 8)
    full = jnp.where(row < 6, state, jnp.where(row == 6, square, along))
    parts = split3(full)
    turned = jnp.where(row < 3, pltpu.roll(state, 5, 0), jnp.where(row < 6, pltpu.roll(state, 3, 0), along))
    swapped = split3(turned * rows_of([0.5] * 6 + [-0.5]))
    scale = rows_of([-2.0] * 3 + [0.0] * 3 + [1.0])
    scale_low = rows_of([-2.0] * 3)
    unit = rows_of([0.0] * 6 + [1.0])
    minus = rows_of([0.0] * 7 + [-0.5])
    own_terms = [(0, 0), (1, 1), (2, 0)]
    plain_terms = [(0, 1), (0, 2), (1, 0)]
    held = [jnp.where(row < 6, parts[p], unit) for p in range(2)]
    home_rows = [parts[p] for p, _ in own_terms] + [held[p] for p, _ in plain_terms]
    dist_rows = [parts[q] * scale_low + unit for _, q in own_terms] + [parts[q] * scale for _, q in plain_terms]
    close_rows = [jnp.where(row < 6, swapped[q], minus) for _, q in own_terms] + [swapped[q] for _, q in plain_terms]
    away_tab[cell, 0] = jnp.concatenate(dist_rows, 0).astype(bf16)
    away_tab[cell, 1] = jnp.concatenate(close_rows, 0).astype(bf16)
    dense = spread(20.0 * rho, 8)
    side = jnp.where(row == 0, dense - 20.0, jnp.where(row == 1, spread(tait_pressure(rho), 8), dense + 20.0))
    row_tab[cell] = side
    if as_home:
        side_parts = split3(side)
        columns = jnp.transpose(jnp.concatenate(home_rows + list(side_parts) + [side_parts[0]], 0)).astype(bf16)
        home_tab[cell] = columns[:, :DEPTH]
        pick = lax.broadcasted_iota(jnp.int32, (DEPTH + 32, 256), 0)
        half = lax.broadcasted_iota(jnp.int32, (DEPTH + 32, 256), 1) // 128
        chosen = (pick >= DEPTH) & (pick < DEPTH + 24) & (pick % 8 == half)
        wide = dot_rows(columns, jnp.where(chosen, 1.0, 0.0).astype(bf16))
        side_tab[cell, 0] = wide[:, :128]
        side_tab[cell, 1] = wide[:, 128:]
    volume = spread(GRAD_SCALE * mass / rho, 8)
    factor = jnp.where(row == 0, 1.0, jnp.where(row == 4, -1.0 / 20.0, pltpu.roll(state, 1, 0)))
    first, second, third = split3(volume * factor)
    none = jnp.zeros((8, 128), f32)
    push_low = jnp.where(row < 4, first, pltpu.roll(third, 4, 0))
    push_high = jnp.where(row < 4, second, 0.0)
    rate_high = jnp.where(row == 4, first, jnp.where(row == 5, pltpu.roll(second, 1, 0), 0.0))
    weight_tab[cell, 0] = jnp.concatenate([push_low, push_high], 0).astype(bf16)
    weight_tab[cell, 1] = jnp.concatenate([none, rate_high], 0).astype(bf16)


def pair_kernel(
    pairs_ref, count_ref, slab_ref, pairs_vec, own, ahead, own_out, ahead_out,
    home_tab, away_tab, side_tab, row_tab, weight_tab, sums, products,
):
    cells = own.shape[1]
    slots = pairs_ref.shape[1]
    tables = (home_tab, away_tab, side_tab, row_tab, weight_tab)
    corner_x = slab_ref[0].astype(f32) + 1.0
    count = count_ref[0]

    def home_of(k):
        at = jnp.minimum(k, slots - 1)
        return jnp.minimum(pairs_ref[0, at], pairs_ref[1, at])

    def away_of(k):
        at = jnp.minimum(k, slots - 1)
        return jnp.maximum(pairs_ref[0, at], pairs_ref[1, at])

    def build(source, offset, as_home):
        def step(at, carry):
            for inner in range(BUILD):
                local = at * BUILD + inner
                build_cell(offset + local, local, source, corner_x, as_home, tables)
            return carry

        lax.fori_loop(0, cells // BUILD, step, 0)

    sums[...] = jnp.zeros_like(sums)
    listed = lax.broadcasted_iota(jnp.int32, (1, slots), 1) < count
    lowest = jnp.minimum(pairs_vec[0:1, :], pairs_vec[1:2, :])
    ahead_homes = jnp.max(jnp.where(listed, lowest, 0)) >= cells
    build(own, 0, True)

    @pl.when(ahead_homes)
    def _():
        build(ahead, cells, True)

    @pl.when(jnp.logical_not(ahead_homes))
    def _():
        build(ahead, cells, False)

    def form(k, slot):
        j = away_of(k)
        both = dot_rows(home_tab[home_of(k)], jnp.concatenate([away_tab[j, 0], away_tab[j, 1]], 1))
        products[slot, 0] = both[:, :128]
        products[slot, 1] = both[:, 128:]

    def factors(k, slot):
        i = home_of(k)
        j = away_of(k)
        dist_sq = jnp.maximum(products[slot, 0], TINY)
        closing = products[slot, 1]
        density_b, pressure_b, raised_b = row_tab[j, 0:1], row_tab[j, 1:2], row_tab[j, 2:3]
        density_a = side_tab[i, 0]
        shell = jnp.maximum(1.0 - dist_sq * lax.rsqrt(dist_sq), 0.0)
        cube = shell * shell * shell
        approach = closing * (density_a + raised_b)
        push = (cube * ((side_tab[i, 1] + pressure_b) + jnp.maximum(approach, 0.0))).astype(bf16)
        dist_n, cube_n = dist_sq.astype(bf16), cube.astype(bf16)
        approach_n, closing_n = approach.astype(bf16), closing.astype(bf16)
        shape = dist_n / (dist_n + bf16(ETA))
        skew = (density_b.astype(bf16) - density_a.astype(bf16)) * (shape + closing_n)
        return push, cube_n * (approach_n - skew), cube_n * (approach_n + skew)

    def gather(k, values):
        push, rate_home, rate_away = values
        i = home_of(k)
        j = away_of(k)
        to_home = dot_lanes(
            jnp.concatenate([weight_tab[j, 0], weight_tab[j, 1]], 1), jnp.concatenate([push, rate_home], 1)
        )
        to_away = dot_rows(
            jnp.concatenate([weight_tab[i, 0], weight_tab[i, 1]], 1), jnp.concatenate([push, rate_away], 0)
        )
        spare = 2 * cells
        sums[jnp.where(k < count, i, spare)] += to_home
        sums[jnp.where((k < count) & (i != j), j, spare)] += to_away

    for k in range(AHEAD - 1):
        form(k, k)

    def turn(at, carry):
        held = None
        for inner in range(GROUP):
            k = at * GROUP + inner
            form(k + AHEAD - 1, (inner + AHEAD - 1) % AHEAD)
            values = factors(k, inner % AHEAD)
            if inner:
                gather(k - 1, held)
            held = values
        gather(at * GROUP + GROUP - 1, held)
        return carry

    lax.fori_loop(0, (count + GROUP - 1) // GROUP, turn, 0)

    def finish(source, offset, out):
        def step(at, carry):
            for inner in range(BUILD):
                local = at * BUILD + inner
                low, high = sums[offset + local, 0:8], sums[offset + local, 8:16]
                state = centred(source, local, corner_x)
                total = low + pltpu.roll(low, 4, 0) + high
                force = (total - pltpu.roll(state, 1, 0) * spread(total[0:1], 8)) / spread(state[6:7], 8)
                for k in range(3):
                    out[k, pl.ds(local, 1), :] = force[k + 1 : k + 2]
                out[3, pl.ds(local, 1), :] = high[4:5] + high[5:6]
            return carry

        lax.fori_loop(0, cells // BUILD, step, 0)

    finish(ahead, cells, ahead_out)
    finish(own, 0, own_out)


def pair_sums(pairs, counts, slab, own, ahead):
    cells = own.shape[1]
    shape = jax.ShapeDtypeStruct((4, cells, 128), f32)
    both = 2 * cells
    return pl.pallas_call(
        pair_kernel,
        out_shape=(shape, shape),
        in_specs=[pl.BlockSpec(memory_space=pltpu.SMEM)] * 3
        + [pl.BlockSpec(memory_space=pltpu.VMEM)]
        + [pl.BlockSpec(memory_space=pltpu.VMEM)] * 2,
        out_specs=[pl.BlockSpec(memory_space=pltpu.VMEM)] * 2,
        scratch_shapes=[
            pltpu.VMEM((both, 128, DEPTH), bf16),
            pltpu.VMEM((both, 2, DEPTH, 128), bf16),
            pltpu.VMEM((both, 2, 128, 128), f32),
            pltpu.VMEM((both, 8, 128), f32),
            pltpu.VMEM((both, 2, 16, 128), bf16),
            pltpu.VMEM((both + 1, 16, 128), f32),
            pltpu.VMEM((AHEAD, 2, 128, 128), f32),
        ],
        compiler_params=pltpu.CompilerParams(vmem_limit_bytes=58 << 20),
        cost_estimate=pl.CostEstimate(flops=4 * 10**9, transcendentals=5 * 10**7, bytes_accessed=2 * 10**6),
    )(pairs, counts, slab, pairs, own, ahead)


def shift(array, by):
    peers = lax.axis_size("slab")
    return lax.ppermute(array, "slab", [(i, i + by) for i in range(peers) if 0 <= i + by < peers])


def copies_of(value, step, ways):
    peers = lax.axis_size("slab")
    return tuple(
        lax.ppermute(value, "slab", [(i, (i + m * step) % peers) for i in range(peers)]) for m in range(1, ways)
    )


def per_device(positions, velocity, density, mass, walls, pairs, counts):
    cells = density.shape[0]
    slab = lax.axis_index("slab")
    state = jnp.concatenate([positions, velocity, density[None], mass[None]], 0)
    arrived = shift(state, -1)
    speed = jnp.max(jnp.sum(velocity * velocity, axis=0).reshape(-1, 8, 128), axis=0)
    peers = lax.axis_size("slab")
    reach = min(WAYS, peers)
    others = copies_of(speed, 1, reach)
    kept, lent = pair_sums(pairs, counts, slab.astype(jnp.int32).reshape(1), state, arrived)
    summed = kept + shift(lent, 1)
    others, _ = lax.optimization_barrier((others, lent))
    speed = functools.reduce(jnp.maximum, others, speed)
    while reach < peers:
        ways = min(WAYS, -(-peers // reach))
        speed = functools.reduce(jnp.maximum, copies_of(speed, reach, ways), speed)
        reach *= ways
    fastest = jnp.max(speed)
    step_size = CFL_NUMBER * SMOOTH / (SOUND + jnp.sqrt(fastest))
    gravity = jnp.array([0.0, 0.0, -9.81], f32)[:, None, None]
    fluid = (walls == 0)[None]
    new_velocity = jnp.where(fluid, velocity + step_size * (summed[:3] + gravity), velocity)
    within = jnp.arange(cells, dtype=jnp.int32)
    corner = jnp.stack(
        [
            jnp.zeros((cells,), f32) + slab.astype(f32),
            (within // GZ).astype(f32),
            (within % GZ).astype(f32),
        ]
    )[:, :, None]
    offsets = positions - corner
    new_offsets = jnp.where(fluid, offsets + step_size * new_velocity, offsets)
    new_density = density + step_size * summed[3]
    return (new_offsets, new_velocity, new_density)


def solution(mesh):
    wide = P(None, ("runs", "slab"), None)
    flat = P(("runs", "slab"), None)
    return jax.shard_map(
        per_device,
        mesh=mesh,
        in_specs=(wide, wide, flat, flat, flat, P(None, ("runs", "slab")), P(("runs", "slab"))),
        out_specs=(wide, wide, flat),
        check_vma=False,
    )
```

```python
import functools
import math

import jax
import jax.numpy as jnp
from jax import lax
from jax.experimental import pallas as pl
from jax.experimental.pallas import tpu as pltpu
from jax.sharding import PartitionSpec as P

GY = 8
GZ = 16
SMOOTH = 0.5
SOUND = 10.0
CFL_NUMBER = 0.25
GRAD_SCALE = -105.0 / (16.0 * math.pi * SMOOTH**5)
ETA = 0.01 * SMOOTH * SMOOTH
TINY = 1e-12
DEPTH = 48
GROUP = 32
AHEAD = 4
BUILD = 8
WAYS = 4
bf16 = jnp.bfloat16
f32 = jnp.float32


def split3(value):
    first = value.astype(bf16).astype(f32)
    rest = value - first
    second = rest.astype(bf16).astype(f32)
    third = (rest - second).astype(bf16).astype(f32)
    return first, second, third


def tait_pressure(density):
    square = density * density
    return SOUND * SOUND / 7.0 * (square * square * square * density - 1.0)


def dot_rows(left, right):
    return lax.dot_general(left, right, (((1,), (0,)), ((), ())), preferred_element_type=f32)


def dot_lanes(left, right):
    return lax.dot_general(left, right, (((1,), (1,)), ((), ())), preferred_element_type=f32)


def spread(row, count):
    return jnp.broadcast_to(row, (count, row.shape[1]))


def rows_of(values):
    row = lax.broadcasted_iota(jnp.int32, (8, 128), 0)
    out = jnp.zeros((8, 128), f32)
    for at, value in enumerate(values):
        if value:
            out = jnp.where(row == at, value, out)
    return out


def centred(source, local, corner_x):
    row = lax.broadcasted_iota(jnp.int32, (8, 128), 0)
    middle = jnp.where(row == 0, corner_x, jnp.where(row == 1, 0.5 * GY, jnp.where(row == 2, 0.5 * GZ, 0.0)))
    return source[:, local, :] - middle


def build_cell(cell, local, source, corner_x, as_home, tables):
    home_tab, away_tab, side_tab, row_tab, weight_tab = tables
    row = lax.broadcasted_iota(jnp.int32, (8, 128), 0)
    state = centred(source, local, corner_x)
    x, y, z, vx, vy, vz, rho, mass = [state[k : k + 1] for k in range(8)]
    square = spread(x * x + y * y + z * z, 8)
    along = spread(x * vx + y * vy + z * vz, 8)
    full = jnp.where(row < 6, state, jnp.where(row == 6, square, along))
    parts = split3(full)
    turned = jnp.where(row < 3, pltpu.roll(state, 5, 0), jnp.where(row < 6, pltpu.roll(state, 3, 0), along))
    swapped = split3(turned * rows_of([0.5] * 6 + [-0.5]))
    scale = rows_of([-2.0] * 3 + [0.0] * 3 + [1.0])
    scale_low = rows_of([-2.0] * 3)
    unit = rows_of([0.0] * 6 + [1.0])
    minus = rows_of([0.0] * 7 + [-0.5])
    own_terms = [(0, 0), (1, 1), (2, 0)]
    plain_terms = [(0, 1), (0, 2), (1, 0)]
    held = [jnp.where(row < 6, parts[p], unit) for p in range(2)]
    home_rows = [parts[p] for p, _ in own_terms] + [held[p] for p, _ in plain_terms]
    dist_rows = [parts[q] * scale_low + unit for _, q in own_terms] + [parts[q] * scale for _, q in plain_terms]
    close_rows = [jnp.where(row < 6, swapped[q], minus) for _, q in own_terms] + [swapped[q] for _, q in plain_terms]
    away_tab[cell, 0] = jnp.concatenate(dist_rows, 0).astype(bf16)
    away_tab[cell, 1] = jnp.concatenate(close_rows, 0).astype(bf16)
    dense = spread(20.0 * rho, 8)
    side = jnp.where(row == 0, dense - 20.0, jnp.where(row == 1, spread(tait_pressure(rho), 8), dense + 20.0))
    row_tab[cell] = side
    if as_home:
        side_parts = split3(side)
        columns = jnp.transpose(jnp.concatenate(home_rows + list(side_parts) + [side_parts[0]], 0)).astype(bf16)
        home_tab[cell] = columns[:, :DEPTH]
        pick = lax.broadcasted_iota(jnp.int32, (DEPTH + 32, 256), 0)
        half = lax.broadcasted_iota(jnp.int32, (DEPTH + 32, 256), 1) // 128
        chosen = (pick >= DEPTH) & (pick < DEPTH + 24) & (pick % 8 == half)
        wide = dot_rows(columns, jnp.where(chosen, 1.0, 0.0).astype(bf16))
        side_tab[cell, 0] = wide[:, :128]
        side_tab[cell, 1] = wide[:, 128:]
    volume = spread(GRAD_SCALE * mass / rho, 8)
    factor = jnp.where(row == 0, 1.0, jnp.where(row == 4, -1.0 / 20.0, pltpu.roll(state, 1, 0)))
    first, second, third = split3(volume * factor)
    none = jnp.zeros((8, 128), f32)
    push_low = jnp.where(row < 4, first, pltpu.roll(third, 4, 0))
    push_high = jnp.where(row < 4, second, 0.0)
    rate_high = jnp.where(row == 4, first, jnp.where(row == 5, pltpu.roll(second, 1, 0), 0.0))
    weight_tab[cell, 0] = jnp.concatenate([push_low, push_high], 0).astype(bf16)
    weight_tab[cell, 1] = jnp.concatenate([none, rate_high], 0).astype(bf16)


def pair_kernel(
    pairs_ref, count_ref, slab_ref, pairs_vec, own, ahead, own_out, ahead_out,
    home_tab, away_tab, side_tab, row_tab, weight_tab, sums, products,
):
    cells = own.shape[1]
    slots = pairs_ref.shape[1]
    tables = (home_tab, away_tab, side_tab, row_tab, weight_tab)
    corner_x = slab_ref[0].astype(f32) + 1.0
    count = count_ref[0]

    def home_of(k):
        at = jnp.minimum(k, slots - 1)
        return jnp.minimum(pairs_ref[0, at], pairs_ref[1, at])

    def away_of(k):
        at = jnp.minimum(k, slots - 1)
        return jnp.maximum(pairs_ref[0, at], pairs_ref[1, at])

    def build(source, offset, as_home):
        def step(at, carry):
            for inner in range(BUILD):
                local = at * BUILD + inner
                build_cell(offset + local, local, source, corner_x, as_home, tables)
            return carry

        lax.fori_loop(0, cells // BUILD, step, 0)

    sums[...] = jnp.zeros_like(sums)
    listed = lax.broadcasted_iota(jnp.int32, (1, slots), 1) < count
    lowest = jnp.minimum(pairs_vec[0:1, :], pairs_vec[1:2, :])
    ahead_homes = jnp.max(jnp.where(listed, lowest, 0)) >= cells
    build(own, 0, True)

    @pl.when(ahead_homes)
    def _():
        build(ahead, cells, True)

    @pl.when(jnp.logical_not(ahead_homes))
    def _():
        build(ahead, cells, False)

    def form(k, slot):
        j = away_of(k)
        both = dot_rows(home_tab[home_of(k)], jnp.concatenate([away_tab[j, 0], away_tab[j, 1]], 1))
        products[slot, 0] = both[:, :128]
        products[slot, 1] = both[:, 128:]

    def factors(k, slot):
        i = home_of(k)
        j = away_of(k)
        dist_sq = jnp.maximum(products[slot, 0], TINY)
        closing = products[slot, 1]
        density_b, pressure_b, raised_b = row_tab[j, 0:1], row_tab[j, 1:2], row_tab[j, 2:3]
        density_a = side_tab[i, 0]
        shell = jnp.maximum(1.0 - dist_sq * lax.rsqrt(dist_sq), 0.0)
        cube = shell * shell * shell
        approach = closing * (density_a + raised_b)
        push = (cube * ((side_tab[i, 1] + pressure_b) + jnp.maximum(approach, 0.0))).astype(bf16)
        dist_n, cube_n = dist_sq.astype(bf16), cube.astype(bf16)
        approach_n, closing_n = approach.astype(bf16), closing.astype(bf16)
        shape = dist_n / (dist_n + bf16(ETA))
        skew = (density_b.astype(bf16) - density_a.astype(bf16)) * (shape + closing_n)
        return push, cube_n * (approach_n - skew), cube_n * (approach_n + skew)

    def gather(k, values):
        push, rate_home, rate_away = values
        i = home_of(k)
        j = away_of(k)
        to_home = dot_lanes(
            jnp.concatenate([weight_tab[j, 0], weight_tab[j, 1]], 1), jnp.concatenate([push, rate_home], 1)
        )
        to_away = dot_rows(
            jnp.concatenate([weight_tab[i, 0], weight_tab[i, 1]], 1), jnp.concatenate([push, rate_away], 0)
        )
        spare = 2 * cells
        sums[jnp.where(k < count, i, spare)] += to_home
        sums[jnp.where((k < count) & (i != j), j, spare)] += to_away

    for k in range(AHEAD - 1):
        form(k, k)

    def turn(at, carry):
        held = None
        for inner in range(GROUP):
            k = at * GROUP + inner
            form(k + AHEAD - 1, (inner + AHEAD - 1) % AHEAD)
            values = factors(k, inner % AHEAD)
            if inner:
                gather(k - 1, held)
            held = values
        gather(at * GROUP + GROUP - 1, held)
        return carry

    lax.fori_loop(0, (count + GROUP - 1) // GROUP, turn, 0)

    def finish(source, offset, out):
        def step(at, carry):
            for inner in range(BUILD):
                local = at * BUILD + inner
                low, high = sums[offset + local, 0:8], sums[offset + local, 8:16]
                state = centred(source, local, corner_x)
                total = low + pltpu.roll(low, 4, 0) + high
                force = (total - pltpu.roll(state, 1, 0) * spread(total[0:1], 8)) / spread(state[6:7], 8)
                for k in range(3):
                    out[k, pl.ds(local, 1), :] = force[k + 1 : k + 2]
                out[3, pl.ds(local, 1), :] = high[4:5] + high[5:6]
            return carry

        lax.fori_loop(0, cells // BUILD, step, 0)

    finish(ahead, cells, ahead_out)
    finish(own, 0, own_out)


def pair_sums(pairs, counts, slab, own, ahead):
    cells = own.shape[1]
    shape = jax.ShapeDtypeStruct((4, cells, 128), f32)
    both = 2 * cells
    return pl.pallas_call(
        pair_kernel,
        out_shape=(shape, shape),
        in_specs=[pl.BlockSpec(memory_space=pltpu.SMEM)] * 3
        + [pl.BlockSpec(memory_space=pltpu.VMEM)]
        + [pl.BlockSpec(memory_space=pltpu.VMEM)] * 2,
        out_specs=[pl.BlockSpec(memory_space=pltpu.VMEM)] * 2,
        scratch_shapes=[
            pltpu.VMEM((both, 128, DEPTH), bf16),
            pltpu.VMEM((both, 2, DEPTH, 128), bf16),
            pltpu.VMEM((both, 2, 128, 128), f32),
            pltpu.VMEM((both, 8, 128), f32),
            pltpu.VMEM((both, 2, 16, 128), bf16),
            pltpu.VMEM((both + 1, 16, 128), f32),
            pltpu.VMEM((AHEAD, 2, 128, 128), f32),
        ],
        compiler_params=pltpu.CompilerParams(vmem_limit_bytes=58 << 20),
        cost_estimate=pl.CostEstimate(flops=4 * 10**9, transcendentals=5 * 10**7, bytes_accessed=2 * 10**6),
    )(pairs, counts, slab, pairs, own, ahead)


def shift(array, by):
    peers = lax.axis_size("slab")
    return lax.ppermute(array, "slab", [(i, i + by) for i in range(peers) if 0 <= i + by < peers])


def copies_of(value, step, ways):
    peers = lax.axis_size("slab")
    return tuple(
        lax.ppermute(value, "slab", [(i, (i + m * step) % peers) for i in range(peers)]) for m in range(1, ways)
    )


def per_device(positions, velocity, density, mass, walls, pairs, counts):
    cells = density.shape[0]
    slab = lax.axis_index("slab")
    state = jnp.concatenate([positions, velocity, density[None], mass[None]], 0)
    arrived = shift(state, -1)
    speed = jnp.max(jnp.sum(velocity * velocity, axis=0).reshape(-1, 8, 128), axis=0)
    peers = lax.axis_size("slab")
    reach = min(WAYS, peers)
    others = copies_of(speed, 1, reach)
    while reach < peers:
        speed = functools.reduce(jnp.maximum, others, speed)
        ways = min(WAYS, -(-peers // reach))
        others = copies_of(speed, reach, ways)
        reach *= ways
    kept, lent = pair_sums(pairs, counts, slab.astype(jnp.int32).reshape(1), state, arrived)
    summed = kept + shift(lent, 1)
    others, _ = lax.optimization_barrier((others, lent))
    fastest = jnp.max(functools.reduce(jnp.maximum, others, speed))
    step_size = CFL_NUMBER * SMOOTH / (SOUND + jnp.sqrt(fastest))
    gravity = jnp.array([0.0, 0.0, -9.81], f32)[:, None, None]
    fluid = (walls == 0)[None]
    new_velocity = jnp.where(fluid, velocity + step_size * (summed[:3] + gravity), velocity)
    within = jnp.arange(cells, dtype=jnp.int32)
    corner = jnp.stack(
        [
            jnp.zeros((cells,), f32) + slab.astype(f32),
            (within // GZ).astype(f32),
            (within % GZ).astype(f32),
        ]
    )[:, :, None]
    offsets = positions - corner
    new_offsets = jnp.where(fluid, offsets + step_size * new_velocity, offsets)
    new_density = density + step_size * summed[3]
    return (new_offsets, new_velocity, new_density)


def solution(mesh):
    wide = P(None, ("runs", "slab"), None)
    flat = P(("runs", "slab"), None)
    return jax.shard_map(
        per_device,
        mesh=mesh,
        in_specs=(wide, wide, flat, flat, flat, P(None, ("runs", "slab")), P(("runs", "slab"))),
        out_specs=(wide, wide, flat),
        check_vma=False,
    )
```

```python
import functools
import math

import jax
import jax.numpy as jnp
from jax import lax
from jax.experimental import pallas as pl
from jax.experimental.pallas import tpu as pltpu
from jax.sharding import PartitionSpec as P

GY = 8
GZ = 16
SMOOTH = 0.5
SOUND = 10.0
CFL_NUMBER = 0.25
GRAD_SCALE = -105.0 / (16.0 * math.pi * SMOOTH**5)
ETA = 0.01 * SMOOTH * SMOOTH
TINY = 1e-12
DEPTH = 48
GROUP = 32
AHEAD = 4
BUILD = 8
WAYS = 4
bf16 = jnp.bfloat16
f32 = jnp.float32


def split3(value):
    first = value.astype(bf16).astype(f32)
    rest = value - first
    second = rest.astype(bf16).astype(f32)
    third = (rest - second).astype(bf16).astype(f32)
    return first, second, third


def tait_pressure(density):
    square = density * density
    return SOUND * SOUND / 7.0 * (square * square * square * density - 1.0)


def dot_rows(left, right):
    return lax.dot_general(left, right, (((1,), (0,)), ((), ())), preferred_element_type=f32)


def dot_lanes(left, right):
    return lax.dot_general(left, right, (((1,), (1,)), ((), ())), preferred_element_type=f32)


def spread(row, count):
    return jnp.broadcast_to(row, (count, row.shape[1]))


def rows_of(values):
    row = lax.broadcasted_iota(jnp.int32, (8, 128), 0)
    out = jnp.zeros((8, 128), f32)
    for at, value in enumerate(values):
        if value:
            out = jnp.where(row == at, value, out)
    return out


def centred(source, local, corner_x):
    row = lax.broadcasted_iota(jnp.int32, (8, 128), 0)
    middle = jnp.where(row == 0, corner_x, jnp.where(row == 1, 0.5 * GY, jnp.where(row == 2, 0.5 * GZ, 0.0)))
    return source[:, local, :] - middle


def build_cell(cell, local, source, corner_x, as_home, tables):
    home_tab, away_tab, side_tab, row_tab, weight_tab = tables
    row = lax.broadcasted_iota(jnp.int32, (8, 128), 0)
    state = centred(source, local, corner_x)
    x, y, z, vx, vy, vz, rho, mass = [state[k : k + 1] for k in range(8)]
    square = spread(x * x + y * y + z * z, 8)
    along = spread(x * vx + y * vy + z * vz, 8)
    full = jnp.where(row < 6, state, jnp.where(row == 6, square, along))
    parts = split3(full)
    turned = jnp.where(row < 3, pltpu.roll(state, 5, 0), jnp.where(row < 6, pltpu.roll(state, 3, 0), along))
    swapped = split3(turned * rows_of([0.5] * 6 + [-0.5]))
    scale = rows_of([-2.0] * 3 + [0.0] * 3 + [1.0])
    scale_low = rows_of([-2.0] * 3)
    unit = rows_of([0.0] * 6 + [1.0])
    minus = rows_of([0.0] * 7 + [-0.5])
    own_terms = [(0, 0), (1, 1), (2, 0)]
    plain_terms = [(0, 1), (0, 2), (1, 0)]
    held = [jnp.where(row < 6, parts[p], unit) for p in range(2)]
    home_rows = [parts[p] for p, _ in own_terms] + [held[p] for p, _ in plain_terms]
    dist_rows = [parts[q] * scale_low + unit for _, q in own_terms] + [parts[q] * scale for _, q in plain_terms]
    close_rows = [jnp.where(row < 6, swapped[q], minus) for _, q in own_terms] + [swapped[q] for _, q in plain_terms]
    away_tab[cell, 0] = jnp.concatenate(dist_rows, 0).astype(bf16)
    away_tab[cell, 1] = jnp.concatenate(close_rows, 0).astype(bf16)
    dense = spread(20.0 * rho, 8)
    side = jnp.where(row == 0, dense - 20.0, jnp.where(row == 1, spread(tait_pressure(rho), 8), dense + 20.0))
    row_tab[cell] = side
    if as_home:
        side_parts = split3(side)
        columns = jnp.transpose(jnp.concatenate(home_rows + list(side_parts) + [side_parts[0]], 0)).astype(bf16)
        home_tab[local] = columns[:, :DEPTH]
        pick = lax.broadcasted_iota(jnp.int32, (DEPTH + 32, 256), 0)
        half = lax.broadcasted_iota(jnp.int32, (DEPTH + 32, 256), 1) // 128
        chosen = (pick >= DEPTH) & (pick < DEPTH + 24) & (pick % 8 == half)
        wide = dot_rows(columns, jnp.where(chosen, 1.0, 0.0).astype(bf16))
        side_tab[local, 0] = wide[:, :128]
        side_tab[local, 1] = wide[:, 128:]
    volume = spread(GRAD_SCALE * mass / rho, 8)
    factor = jnp.where(row == 0, 1.0, jnp.where(row == 4, -1.0 / 20.0, pltpu.roll(state, 1, 0)))
    first, second, third = split3(volume * factor)
    none = jnp.zeros((8, 128), f32)
    push_low = jnp.where(row < 4, first, pltpu.roll(third, 4, 0))
    push_high = jnp.where(row < 4, second, 0.0)
    rate_high = jnp.where(row == 4, first, jnp.where(row == 5, pltpu.roll(second, 1, 0), 0.0))
    weight_tab[cell, 0] = jnp.concatenate([push_low, push_high], 0).astype(bf16)
    weight_tab[cell, 1] = jnp.concatenate([none, rate_high], 0).astype(bf16)


def pair_kernel(
    pairs_ref, count_ref, slab_ref, pairs_vec, own, ahead, own_out, ahead_out,
    home_tab, away_tab, side_tab, row_tab, weight_tab, sums, products,
):
    cells = own.shape[1]
    slots = pairs_ref.shape[1]
    tables = (home_tab, away_tab, side_tab, row_tab, weight_tab)
    corner_x = slab_ref[0].astype(f32) + 1.0
    count = count_ref[0]

    def home_of(k):
        at = jnp.minimum(k, slots - 1)
        return jnp.minimum(pairs_ref[0, at], pairs_ref[1, at])

    def away_of(k):
        at = jnp.minimum(k, slots - 1)
        return jnp.maximum(pairs_ref[0, at], pairs_ref[1, at])

    def build(source, offset, as_home):
        def step(at, carry):
            for inner in range(BUILD):
                local = at * BUILD + inner
                build_cell(offset + local, local, source, corner_x, as_home, tables)
            return carry

        lax.fori_loop(0, cells // BUILD, step, 0)

    sums[...] = jnp.zeros_like(sums)
    listed = lax.broadcasted_iota(jnp.int32, (1, slots), 1) < count
    lowest = jnp.minimum(pairs_vec[0:1, :], pairs_vec[1:2, :])
    ahead_homes = jnp.max(jnp.where(listed, lowest, 0)) >= cells
    build(own, 0, True)

    build(ahead, cells, False)

    def slot_of(k, base):
        return jnp.clip(home_of(k) - base, 0, cells - 1)

    def form(k, slot, base):
        j = away_of(k)
        both = dot_rows(home_tab[slot_of(k, base)], jnp.concatenate([away_tab[j, 0], away_tab[j, 1]], 1))
        products[slot, 0] = both[:, :128]
        products[slot, 1] = both[:, 128:]

    def factors(k, slot, base):
        i = slot_of(k, base)
        j = away_of(k)
        dist_sq = jnp.maximum(products[slot, 0], TINY)
        closing = products[slot, 1]
        density_b, pressure_b, raised_b = row_tab[j, 0:1], row_tab[j, 1:2], row_tab[j, 2:3]
        density_a = side_tab[i, 0]
        shell = jnp.maximum(1.0 - dist_sq * lax.rsqrt(dist_sq), 0.0)
        cube = shell * shell * shell
        approach = closing * (density_a + raised_b)
        push = (cube * ((side_tab[i, 1] + pressure_b) + jnp.maximum(approach, 0.0))).astype(bf16)
        dist_n, cube_n = dist_sq.astype(bf16), cube.astype(bf16)
        approach_n, closing_n = approach.astype(bf16), closing.astype(bf16)
        shape = dist_n / (dist_n + bf16(ETA))
        skew = (density_b.astype(bf16) - density_a.astype(bf16)) * (shape + closing_n)
        return push, cube_n * (approach_n - skew), cube_n * (approach_n + skew)

    def gather(k, values, base):
        push, rate_home, rate_away = values
        i = home_of(k)
        j = away_of(k)
        to_home = dot_lanes(
            jnp.concatenate([weight_tab[j, 0], weight_tab[j, 1]], 1), jnp.concatenate([push, rate_home], 1)
        )
        to_away = dot_rows(
            jnp.concatenate([weight_tab[i, 0], weight_tab[i, 1]], 1), jnp.concatenate([push, rate_away], 0)
        )
        spare = 2 * cells
        live = (k < count) & (i >= base) & (i < base + cells)
        sums[jnp.where(live, i, spare)] += to_home
        sums[jnp.where(live & (i != j), j, spare)] += to_away

    def sweep(at_pass, carry):
        base = at_pass * cells

        @pl.when(at_pass > 0)
        def _():
            build(ahead, cells, True)

        for k in range(AHEAD - 1):
            form(k, k, base)

        def turn(at, inner_carry):
            held = None
            for inner in range(GROUP):
                k = at * GROUP + inner
                form(k + AHEAD - 1, (inner + AHEAD - 1) % AHEAD, base)
                values = factors(k, inner % AHEAD, base)
                if inner:
                    gather(k - 1, held, base)
                held = values
            gather(at * GROUP + GROUP - 1, held, base)
            return inner_carry

        lax.fori_loop(0, (count + GROUP - 1) // GROUP, turn, 0)
        return carry

    lax.fori_loop(0, jnp.where(ahead_homes, 2, 1), sweep, 0)

    def finish(source, offset, out):
        def step(at, carry):
            for inner in range(BUILD):
                local = at * BUILD + inner
                low, high = sums[offset + local, 0:8], sums[offset + local, 8:16]
                state = centred(source, local, corner_x)
                total = low + pltpu.roll(low, 4, 0) + high
                force = (total - pltpu.roll(state, 1, 0) * spread(total[0:1], 8)) / spread(state[6:7], 8)
                for k in range(3):
                    out[k, pl.ds(local, 1), :] = force[k + 1 : k + 2]
                out[3, pl.ds(local, 1), :] = high[4:5] + high[5:6]
            return carry

        lax.fori_loop(0, cells // BUILD, step, 0)

    finish(ahead, cells, ahead_out)
    finish(own, 0, own_out)


def pair_sums(pairs, counts, slab, own, ahead):
    cells = own.shape[1]
    shape = jax.ShapeDtypeStruct((4, cells, 128), f32)
    both = 2 * cells
    return pl.pallas_call(
        pair_kernel,
        out_shape=(shape, shape),
        in_specs=[pl.BlockSpec(memory_space=pltpu.SMEM)] * 3
        + [pl.BlockSpec(memory_space=pltpu.VMEM)]
        + [pl.BlockSpec(memory_space=pltpu.VMEM)] * 2,
        out_specs=[pl.BlockSpec(memory_space=pltpu.VMEM)] * 2,
        scratch_shapes=[
            pltpu.VMEM((cells, 128, DEPTH), bf16),
            pltpu.VMEM((both, 2, DEPTH, 128), bf16),
            pltpu.VMEM((cells, 2, 128, 128), f32),
            pltpu.VMEM((both, 8, 128), f32),
            pltpu.VMEM((both, 2, 16, 128), bf16),
            pltpu.VMEM((both + 1, 16, 128), f32),
            pltpu.VMEM((AHEAD, 2, 128, 128), f32),
        ],
        compiler_params=pltpu.CompilerParams(vmem_limit_bytes=36 << 20),
        cost_estimate=pl.CostEstimate(flops=4 * 10**9, transcendentals=5 * 10**7, bytes_accessed=2 * 10**6),
    )(pairs, counts, slab, pairs, own, ahead)


def shift(array, by):
    peers = lax.axis_size("slab")
    return lax.ppermute(array, "slab", [(i, i + by) for i in range(peers) if 0 <= i + by < peers])


def copies_of(value, step, ways):
    peers = lax.axis_size("slab")
    return tuple(
        lax.ppermute(value, "slab", [(i, (i + m * step) % peers) for i in range(peers)]) for m in range(1, ways)
    )


def per_device(positions, velocity, density, mass, walls, pairs, counts):
    cells = density.shape[0]
    slab = lax.axis_index("slab")
    state = jnp.concatenate([positions, velocity, density[None], mass[None]], 0)
    arrived = shift(state, -1)
    speed = jnp.max(jnp.sum(velocity * velocity, axis=0).reshape(-1, 8, 128), axis=0)
    peers = lax.axis_size("slab")
    reach = min(WAYS, peers)
    others = copies_of(speed, 1, reach)
    kept, lent = pair_sums(pairs, counts, slab.astype(jnp.int32).reshape(1), state, arrived)
    summed = kept + shift(lent, 1)
    others, _ = lax.optimization_barrier((others, lent))
    speed = functools.reduce(jnp.maximum, others, speed)
    while reach < peers:
        ways = min(WAYS, -(-peers // reach))
        speed = functools.reduce(jnp.maximum, copies_of(speed, reach, ways), speed)
        reach *= ways
    fastest = jnp.max(speed)
    step_size = CFL_NUMBER * SMOOTH / (SOUND + jnp.sqrt(fastest))
    gravity = jnp.array([0.0, 0.0, -9.81], f32)[:, None, None]
    fluid = (walls == 0)[None]
    new_velocity = jnp.where(fluid, velocity + step_size * (summed[:3] + gravity), velocity)
    within = jnp.arange(cells, dtype=jnp.int32)
    corner = jnp.stack(
        [
            jnp.zeros((cells,), f32) + slab.astype(f32),
            (within // GZ).astype(f32),
            (within % GZ).astype(f32),
        ]
    )[:, :, None]
    offsets = positions - corner
    new_offsets = jnp.where(fluid, offsets + step_size * new_velocity, offsets)
    new_density = density + step_size * summed[3]
    return (new_offsets, new_velocity, new_density)


def solution(mesh):
    wide = P(None, ("runs", "slab"), None)
    flat = P(("runs", "slab"), None)
    return jax.shard_map(
        per_device,
        mesh=mesh,
        in_specs=(wide, wide, flat, flat, flat, P(None, ("runs", "slab")), P(("runs", "slab"))),
        out_specs=(wide, wide, flat),
        check_vma=False,
    )
```

```python
import functools
import math

import jax
import jax.numpy as jnp
from jax import lax
from jax.experimental import pallas as pl
from jax.experimental.pallas import tpu as pltpu
from jax.sharding import PartitionSpec as P

GY = 8
GZ = 16
SMOOTH = 0.5
SOUND = 10.0
CFL_NUMBER = 0.25
GRAD_SCALE = -105.0 / (16.0 * math.pi * SMOOTH**5)
ETA = 0.01 * SMOOTH * SMOOTH
TINY = 1e-12
DEPTH = 48
GROUP = 32
AHEAD = 4
BUILD = 8
WAYS = 4
bf16 = jnp.bfloat16
f32 = jnp.float32


def split3(value):
    first = value.astype(bf16).astype(f32)
    rest = value - first
    second = rest.astype(bf16).astype(f32)
    third = (rest - second).astype(bf16).astype(f32)
    return first, second, third


def tait_pressure(density):
    square = density * density
    return SOUND * SOUND / 7.0 * (square * square * square * density - 1.0)


def dot_rows(left, right):
    return lax.dot_general(left, right, (((1,), (0,)), ((), ())), preferred_element_type=f32)


def dot_lanes(left, right):
    return lax.dot_general(left, right, (((1,), (1,)), ((), ())), preferred_element_type=f32)


def spread(row, count):
    return jnp.broadcast_to(row, (count, row.shape[1]))


def rows_of(values):
    row = lax.broadcasted_iota(jnp.int32, (8, 128), 0)
    out = jnp.zeros((8, 128), f32)
    for at, value in enumerate(values):
        if value:
            out = jnp.where(row == at, value, out)
    return out


def centred(source, local, corner_x):
    row = lax.broadcasted_iota(jnp.int32, (8, 128), 0)
    middle = jnp.where(row == 0, corner_x, jnp.where(row == 1, 0.5 * GY, jnp.where(row == 2, 0.5 * GZ, 0.0)))
    return source[:, local, :] - middle


def build_cell(cell, local, source, corner_x, as_home, tables):
    home_tab, away_tab, side_tab, row_tab, weight_tab = tables
    row = lax.broadcasted_iota(jnp.int32, (8, 128), 0)
    state = centred(source, local, corner_x)
    x, y, z, vx, vy, vz, rho, mass = [state[k : k + 1] for k in range(8)]
    square = spread(x * x + y * y + z * z, 8)
    along = spread(x * vx + y * vy + z * vz, 8)
    full = jnp.where(row < 6, state, jnp.where(row == 6, square, along))
    parts = split3(full)
    turned = jnp.where(row < 3, pltpu.roll(state, 5, 0), jnp.where(row < 6, pltpu.roll(state, 3, 0), along))
    swapped = split3(turned * rows_of([0.5] * 6 + [-0.5]))
    scale = rows_of([-2.0] * 3 + [0.0] * 3 + [1.0])
    scale_low = rows_of([-2.0] * 3)
    unit = rows_of([0.0] * 6 + [1.0])
    minus = rows_of([0.0] * 7 + [-0.5])
    own_terms = [(0, 0), (1, 1), (2, 0)]
    plain_terms = [(0, 1), (0, 2), (1, 0)]
    held = [jnp.where(row < 6, parts[p], unit) for p in range(2)]
    home_rows = [parts[p] for p, _ in own_terms] + [held[p] for p, _ in plain_terms]
    dist_rows = [parts[q] * scale_low + unit for _, q in own_terms] + [parts[q] * scale for _, q in plain_terms]
    close_rows = [jnp.where(row < 6, swapped[q], minus) for _, q in own_terms] + [swapped[q] for _, q in plain_terms]
    away_tab[cell, 0] = jnp.concatenate(dist_rows, 0).astype(bf16)
    away_tab[cell, 1] = jnp.concatenate(close_rows, 0).astype(bf16)
    dense = spread(20.0 * rho, 8)
    side = jnp.where(row == 0, dense - 20.0, jnp.where(row == 1, spread(tait_pressure(rho), 8), dense + 20.0))
    row_tab[cell] = side
    if as_home:
        side_parts = split3(side)
        columns = jnp.transpose(jnp.concatenate(home_rows + list(side_parts) + [side_parts[0]], 0)).astype(bf16)
        home_tab[local] = columns[:, :DEPTH]
        pick = lax.broadcasted_iota(jnp.int32, (DEPTH + 32, 256), 0)
        half = lax.broadcasted_iota(jnp.int32, (DEPTH + 32, 256), 1) // 128
        chosen = (pick >= DEPTH) & (pick < DEPTH + 24) & (pick % 8 == half)
        wide = dot_rows(columns, jnp.where(chosen, 1.0, 0.0).astype(bf16))
        side_tab[local, 0] = wide[:, :128]
        side_tab[local, 1] = wide[:, 128:]
    volume = spread(GRAD_SCALE * mass / rho, 8)
    factor = jnp.where(row == 0, 1.0, jnp.where(row == 4, -1.0 / 20.0, pltpu.roll(state, 1, 0)))
    first, second, third = split3(volume * factor)
    none = jnp.zeros((8, 128), f32)
    push_low = jnp.where(row < 4, first, pltpu.roll(third, 4, 0))
    push_high = jnp.where(row < 4, second, 0.0)
    rate_high = jnp.where(row == 4, first, jnp.where(row == 5, pltpu.roll(second, 1, 0), 0.0))
    weight_tab[cell, 0] = jnp.concatenate([push_low, push_high], 0).astype(bf16)
    weight_tab[cell, 1] = jnp.concatenate([none, rate_high], 0).astype(bf16)


def pair_kernel(
    pairs_ref, count_ref, slab_ref, pairs_vec, own, ahead, own_out, ahead_out,
    home_tab, away_tab, side_tab, row_tab, weight_tab, sums, products,
):
    cells = own.shape[1]
    slots = pairs_ref.shape[1]
    tables = (home_tab, away_tab, side_tab, row_tab, weight_tab)
    corner_x = slab_ref[0].astype(f32) + 1.0
    count = count_ref[0]

    def home_of(k):
        at = jnp.minimum(k, slots - 1)
        return jnp.minimum(pairs_ref[0, at], pairs_ref[1, at])

    def away_of(k):
        at = jnp.minimum(k, slots - 1)
        return jnp.maximum(pairs_ref[0, at], pairs_ref[1, at])

    def build(source, offset, as_home):
        def step(at, carry):
            for inner in range(BUILD):
                local = at * BUILD + inner
                build_cell(offset + local, local, source, corner_x, as_home, tables)
            return carry

        lax.fori_loop(0, cells // BUILD, step, 0)

    sums[...] = jnp.zeros_like(sums)
    listed = lax.broadcasted_iota(jnp.int32, (1, slots), 1) < count
    lowest = jnp.minimum(pairs_vec[0:1, :], pairs_vec[1:2, :])
    ahead_homes = jnp.max(jnp.where(listed, lowest, 0)) >= cells
    build(own, 0, True)

    build(ahead, cells, False)

    def slot_of(k, base):
        return jnp.clip(home_of(k) - base, 0, cells - 1)

    def form(k, slot, base):
        j = away_of(k)
        both = dot_rows(home_tab[slot_of(k, base)], jnp.concatenate([away_tab[j, 0], away_tab[j, 1]], 1))
        products[slot, 0] = both[:, :128]
        products[slot, 1] = both[:, 128:]

    def factors(k, slot, base):
        i = slot_of(k, base)
        j = away_of(k)
        dist_sq = jnp.maximum(products[slot, 0], TINY)
        closing = products[slot, 1]
        density_b, pressure_b, raised_b = row_tab[j, 0:1], row_tab[j, 1:2], row_tab[j, 2:3]
        density_a = side_tab[i, 0]
        shell = jnp.maximum(1.0 - dist_sq * lax.rsqrt(dist_sq), 0.0)
        cube = shell * shell * shell
        approach = closing * (density_a + raised_b)
        push = (cube * ((side_tab[i, 1] + pressure_b) + jnp.maximum(approach, 0.0))).astype(bf16)
        dist_n, cube_n = dist_sq.astype(bf16), cube.astype(bf16)
        approach_n, closing_n = approach.astype(bf16), closing.astype(bf16)
        shape = dist_n / (dist_n + bf16(ETA))
        skew = (density_b.astype(bf16) - density_a.astype(bf16)) * (shape + closing_n)
        return push, cube_n * (approach_n - skew), cube_n * (approach_n + skew)

    def gather(k, values, base):
        push, rate_home, rate_away = values
        i = home_of(k)
        j = away_of(k)
        to_home = dot_lanes(
            jnp.concatenate([weight_tab[j, 0], weight_tab[j, 1]], 1), jnp.concatenate([push, rate_home], 1)
        )
        to_away = dot_rows(
            jnp.concatenate([weight_tab[i, 0], weight_tab[i, 1]], 1), jnp.concatenate([push, rate_away], 0)
        )
        spare = 2 * cells
        live = (k < count) & (i >= base) & (i < base + cells)
        sums[jnp.where(live, i, spare)] += to_home
        sums[jnp.where(live & (i != j), j, spare)] += to_away

    def sweep(at_pass, carry):
        base = at_pass * cells

        @pl.when(at_pass > 0)
        def _():
            build(ahead, cells, True)

        for k in range(AHEAD - 1):
            form(k, k, base)

        def turn(at, inner_carry):
            held = None
            for inner in range(GROUP):
                k = at * GROUP + inner
                form(k + AHEAD - 1, (inner + AHEAD - 1) % AHEAD, base)
                values = factors(k, inner % AHEAD, base)
                if inner:
                    gather(k - 1, held, base)
                held = values
            gather(at * GROUP + GROUP - 1, held, base)
            return inner_carry

        lax.fori_loop(0, (count + GROUP - 1) // GROUP, turn, 0)
        return carry

    lax.fori_loop(0, jnp.where(ahead_homes, 2, 1), sweep, 0)

    def finish(source, offset, out):
        def step(at, carry):
            for inner in range(BUILD):
                local = at * BUILD + inner
                low, high = sums[offset + local, 0:8], sums[offset + local, 8:16]
                state = centred(source, local, corner_x)
                total = low + pltpu.roll(low, 4, 0) + high
                force = (total - pltpu.roll(state, 1, 0) * spread(total[0:1], 8)) / spread(state[6:7], 8)
                for k in range(3):
                    out[k, pl.ds(local, 1), :] = force[k + 1 : k + 2]
                out[3, pl.ds(local, 1), :] = high[4:5] + high[5:6]
            return carry

        lax.fori_loop(0, cells // BUILD, step, 0)

    finish(ahead, cells, ahead_out)
    finish(own, 0, own_out)


def pair_sums(pairs, counts, slab, own, ahead):
    cells = own.shape[1]
    shape = jax.ShapeDtypeStruct((4, cells, 128), f32)
    both = 2 * cells
    return pl.pallas_call(
        pair_kernel,
        out_shape=(shape, shape),
        in_specs=[pl.BlockSpec(memory_space=pltpu.SMEM)] * 3
        + [pl.BlockSpec(memory_space=pltpu.VMEM)]
        + [pl.BlockSpec(memory_space=pltpu.VMEM)] * 2,
        out_specs=[pl.BlockSpec(memory_space=pltpu.VMEM)] * 2,
        scratch_shapes=[
            pltpu.VMEM((cells, 128, DEPTH), bf16),
            pltpu.VMEM((both, 2, DEPTH, 128), bf16),
            pltpu.VMEM((cells, 2, 128, 128), f32),
            pltpu.VMEM((both, 8, 128), f32),
            pltpu.VMEM((both, 2, 16, 128), bf16),
            pltpu.VMEM((both + 1, 16, 128), f32),
            pltpu.VMEM((AHEAD, 2, 128, 128), f32),
        ],
        compiler_params=pltpu.CompilerParams(vmem_limit_bytes=36 << 20),
        cost_estimate=pl.CostEstimate(flops=4 * 10**9, transcendentals=5 * 10**7, bytes_accessed=2 * 10**6),
    )(pairs, counts, slab, pairs, own, ahead)


def shift(array, by):
    peers = lax.axis_size("slab")
    return lax.ppermute(array, "slab", [(i, i + by) for i in range(peers) if 0 <= i + by < peers])


def copies_of(value, step, ways):
    peers = lax.axis_size("slab")
    return tuple(
        lax.ppermute(value, "slab", [(i, (i + m * step) % peers) for i in range(peers)]) for m in range(1, ways)
    )


def per_device(positions, velocity, density, mass, walls, pairs, counts):
    cells = density.shape[0]
    slab = lax.axis_index("slab")
    state = lax.optimization_barrier(jnp.concatenate([positions, velocity, density[None], mass[None]], 0))
    arrived = shift(state, -1)
    speed = jnp.max(jnp.sum(velocity * velocity, axis=0).reshape(-1, 8, 128), axis=0)
    peers = lax.axis_size("slab")
    reach = min(WAYS, peers)
    others = copies_of(speed, 1, reach)
    kept, lent = pair_sums(pairs, counts, slab.astype(jnp.int32).reshape(1), state, arrived)
    summed = kept + shift(lent, 1)
    others, _ = lax.optimization_barrier((others, lent))
    speed = functools.reduce(jnp.maximum, others, speed)
    while reach < peers:
        ways = min(WAYS, -(-peers // reach))
        speed = functools.reduce(jnp.maximum, copies_of(speed, reach, ways), speed)
        reach *= ways
    fastest = jnp.max(speed)
    step_size = CFL_NUMBER * SMOOTH / (SOUND + jnp.sqrt(fastest))
    gravity = jnp.array([0.0, 0.0, -9.81], f32)[:, None, None]
    fluid = (walls == 0)[None]
    new_velocity = jnp.where(fluid, state[3:6] + step_size * (summed[:3] + gravity), state[3:6])
    within = jnp.arange(cells, dtype=jnp.int32)
    corner = jnp.stack(
        [
            jnp.zeros((cells,), f32) + slab.astype(f32),
            (within // GZ).astype(f32),
            (within % GZ).astype(f32),
        ]
    )[:, :, None]
    offsets = state[:3] - corner
    new_offsets = jnp.where(fluid, offsets + step_size * new_velocity, offsets)
    new_density = state[6] + step_size * summed[3]
    return (new_offsets, new_velocity, new_density)


def solution(mesh):
    wide = P(None, ("runs", "slab"), None)
    flat = P(("runs", "slab"), None)
    return jax.shard_map(
        per_device,
        mesh=mesh,
        in_specs=(wide, wide, flat, flat, flat, P(None, ("runs", "slab")), P(("runs", "slab"))),
        out_specs=(wide, wide, flat),
        check_vma=False,
    )
```

```python
import functools
import math

import jax
import jax.numpy as jnp
from jax import lax
from jax.experimental import pallas as pl
from jax.experimental.pallas import tpu as pltpu
from jax.sharding import PartitionSpec as P

GY = 8
GZ = 16
SMOOTH = 0.5
SOUND = 10.0
CFL_NUMBER = 0.25
GRAD_SCALE = -105.0 / (16.0 * math.pi * SMOOTH**5)
ETA = 0.01 * SMOOTH * SMOOTH
TINY = 1e-12
DEPTH = 48
GROUP = 32
AHEAD = 4
BUILD = 8
FIRST_WAYS = 6
LATER_WAYS = 3
bf16 = jnp.bfloat16
f32 = jnp.float32


def split3(value):
    first = value.astype(bf16).astype(f32)
    rest = value - first
    second = rest.astype(bf16).astype(f32)
    third = (rest - second).astype(bf16).astype(f32)
    return first, second, third


def tait_pressure(density):
    square = density * density
    return SOUND * SOUND / 7.0 * (square * square * square * density - 1.0)


def dot_rows(left, right):
    return lax.dot_general(left, right, (((1,), (0,)), ((), ())), preferred_element_type=f32)


def dot_lanes(left, right):
    return lax.dot_general(left, right, (((1,), (1,)), ((), ())), preferred_element_type=f32)


def spread(row, count):
    return jnp.broadcast_to(row, (count, row.shape[1]))


def rows_of(values):
    row = lax.broadcasted_iota(jnp.int32, (8, 128), 0)
    out = jnp.zeros((8, 128), f32)
    for at, value in enumerate(values):
        if value:
            out = jnp.where(row == at, value, out)
    return out


def centred(source, local, corner_x):
    row = lax.broadcasted_iota(jnp.int32, (8, 128), 0)
    middle = jnp.where(row == 0, corner_x, jnp.where(row == 1, 0.5 * GY, jnp.where(row == 2, 0.5 * GZ, 0.0)))
    return source[:, local, :] - middle


def build_cell(cell, local, source, corner_x, as_home, tables):
    home_tab, away_tab, side_tab, row_tab, weight_tab = tables
    row = lax.broadcasted_iota(jnp.int32, (8, 128), 0)
    state = centred(source, local, corner_x)
    x, y, z, vx, vy, vz, rho, mass = [state[k : k + 1] for k in range(8)]
    square = spread(x * x + y * y + z * z, 8)
    along = spread(x * vx + y * vy + z * vz, 8)
    full = jnp.where(row < 6, state, jnp.where(row == 6, square, along))
    parts = split3(full)
    turned = jnp.where(row < 3, pltpu.roll(state, 5, 0), jnp.where(row < 6, pltpu.roll(state, 3, 0), along))
    swapped = split3(turned * rows_of([0.5] * 6 + [-0.5]))
    scale = rows_of([-2.0] * 3 + [0.0] * 3 + [1.0])
    scale_low = rows_of([-2.0] * 3)
    unit = rows_of([0.0] * 6 + [1.0])
    minus = rows_of([0.0] * 7 + [-0.5])
    own_terms = [(0, 0), (1, 1), (2, 0)]
    plain_terms = [(0, 1), (0, 2), (1, 0)]
    held = [jnp.where(row < 6, parts[p], unit) for p in range(2)]
    home_rows = [parts[p] for p, _ in own_terms] + [held[p] for p, _ in plain_terms]
    dist_rows = [parts[q] * scale_low + unit for _, q in own_terms] + [parts[q] * scale for _, q in plain_terms]
    close_rows = [jnp.where(row < 6, swapped[q], minus) for _, q in own_terms] + [swapped[q] for _, q in plain_terms]
    away_tab[cell, 0] = jnp.concatenate(dist_rows, 0).astype(bf16)
    away_tab[cell, 1] = jnp.concatenate(close_rows, 0).astype(bf16)
    dense = spread(20.0 * rho, 8)
    side = jnp.where(row == 0, dense - 20.0, jnp.where(row == 1, spread(tait_pressure(rho), 8), dense + 20.0))
    row_tab[cell] = side
    if as_home:
        side_parts = split3(side)
        columns = jnp.transpose(jnp.concatenate(home_rows + list(side_parts) + [side_parts[0]], 0)).astype(bf16)
        home_tab[local] = columns[:, :DEPTH]
        pick = lax.broadcasted_iota(jnp.int32, (DEPTH + 32, 256), 0)
        half = lax.broadcasted_iota(jnp.int32, (DEPTH + 32, 256), 1) // 128
        chosen = (pick >= DEPTH) & (pick < DEPTH + 24) & (pick % 8 == half)
        wide = dot_rows(columns, jnp.where(chosen, 1.0, 0.0).astype(bf16))
        side_tab[local, 0] = wide[:, :128]
        side_tab[local, 1] = wide[:, 128:]
    volume = spread(GRAD_SCALE * mass / rho, 8)
    factor = jnp.where(row == 0, 1.0, jnp.where(row == 4, -1.0 / 20.0, pltpu.roll(state, 1, 0)))
    first, second, third = split3(volume * factor)
    none = jnp.zeros((8, 128), f32)
    push_low = jnp.where(row < 4, first, pltpu.roll(third, 4, 0))
    push_high = jnp.where(row < 4, second, 0.0)
    rate_high = jnp.where(row == 4, first, jnp.where(row == 5, pltpu.roll(second, 1, 0), 0.0))
    weight_tab[cell, 0] = jnp.concatenate([push_low, push_high], 0).astype(bf16)
    weight_tab[cell, 1] = jnp.concatenate([none, rate_high], 0).astype(bf16)


def pair_kernel(
    pairs_ref, count_ref, slab_ref, pairs_vec, own, ahead, own_out, ahead_out,
    home_tab, away_tab, side_tab, row_tab, weight_tab, sums, products,
):
    cells = own.shape[1]
    slots = pairs_ref.shape[1]
    tables = (home_tab, away_tab, side_tab, row_tab, weight_tab)
    corner_x = slab_ref[0].astype(f32) + 1.0
    count = count_ref[0]

    def home_of(k):
        at = jnp.minimum(k, slots - 1)
        return jnp.minimum(pairs_ref[0, at], pairs_ref[1, at])

    def away_of(k):
        at = jnp.minimum(k, slots - 1)
        return jnp.maximum(pairs_ref[0, at], pairs_ref[1, at])

    def build(source, offset, as_home):
        def step(at, carry):
            for inner in range(BUILD):
                local = at * BUILD + inner
                build_cell(offset + local, local, source, corner_x, as_home, tables)
            return carry

        lax.fori_loop(0, cells // BUILD, step, 0)

    sums[...] = jnp.zeros_like(sums)
    listed = lax.broadcasted_iota(jnp.int32, (1, slots), 1) < count
    lowest = jnp.minimum(pairs_vec[0:1, :], pairs_vec[1:2, :])
    ahead_homes = jnp.max(jnp.where(listed, lowest, 0)) >= cells
    build(own, 0, True)

    build(ahead, cells, False)

    def slot_of(k, base):
        return jnp.clip(home_of(k) - base, 0, cells - 1)

    def form(k, slot, base):
        j = away_of(k)
        both = dot_rows(home_tab[slot_of(k, base)], jnp.concatenate([away_tab[j, 0], away_tab[j, 1]], 1))
        products[slot, 0] = both[:, :128]
        products[slot, 1] = both[:, 128:]

    def factors(k, slot, base):
        i = slot_of(k, base)
        j = away_of(k)
        dist_sq = jnp.maximum(products[slot, 0], TINY)
        closing = products[slot, 1]
        density_b, pressure_b, raised_b = row_tab[j, 0:1], row_tab[j, 1:2], row_tab[j, 2:3]
        density_a = side_tab[i, 0]
        shell = jnp.maximum(1.0 - dist_sq * lax.rsqrt(dist_sq), 0.0)
        cube = shell * shell * shell
        approach = closing * (density_a + raised_b)
        push = (cube * ((side_tab[i, 1] + pressure_b) + jnp.maximum(approach, 0.0))).astype(bf16)
        dist_n, cube_n = dist_sq.astype(bf16), cube.astype(bf16)
        approach_n, closing_n = approach.astype(bf16), closing.astype(bf16)
        shape = dist_n / (dist_n + bf16(ETA))
        skew = (density_b.astype(bf16) - density_a.astype(bf16)) * (shape + closing_n)
        return push, cube_n * (approach_n - skew), cube_n * (approach_n + skew)

    def gather(k, values, base):
        push, rate_home, rate_away = values
        i = home_of(k)
        j = away_of(k)
        to_home = dot_lanes(
            jnp.concatenate([weight_tab[j, 0], weight_tab[j, 1]], 1), jnp.concatenate([push, rate_home], 1)
        )
        to_away = dot_rows(
            jnp.concatenate([weight_tab[i, 0], weight_tab[i, 1]], 1), jnp.concatenate([push, rate_away], 0)
        )
        spare = 2 * cells
        live = (k < count) & (i >= base) & (i < base + cells)
        sums[jnp.where(live, i, spare)] += to_home
        sums[jnp.where(live & (i != j), j, spare)] += to_away

    def sweep(at_pass, carry):
        base = at_pass * cells

        @pl.when(at_pass > 0)
        def _():
            build(ahead, cells, True)

        for k in range(AHEAD - 1):
            form(k, k, base)

        def turn(at, inner_carry):
            held = None
            for inner in range(GROUP):
                k = at * GROUP + inner
                form(k + AHEAD - 1, (inner + AHEAD - 1) % AHEAD, base)
                values = factors(k, inner % AHEAD, base)
                if inner:
                    gather(k - 1, held, base)
                held = values
            gather(at * GROUP + GROUP - 1, held, base)
            return inner_carry

        lax.fori_loop(0, (count + GROUP - 1) // GROUP, turn, 0)
        return carry

    lax.fori_loop(0, jnp.where(ahead_homes, 2, 1), sweep, 0)

    def finish(source, offset, out):
        def step(at, carry):
            for inner in range(BUILD):
                local = at * BUILD + inner
                low, high = sums[offset + local, 0:8], sums[offset + local, 8:16]
                state = centred(source, local, corner_x)
                total = low + pltpu.roll(low, 4, 0) + high
                force = (total - pltpu.roll(state, 1, 0) * spread(total[0:1], 8)) / spread(state[6:7], 8)
                for k in range(3):
                    out[k, pl.ds(local, 1), :] = force[k + 1 : k + 2]
                out[3, pl.ds(local, 1), :] = high[4:5] + high[5:6]
            return carry

        lax.fori_loop(0, cells // BUILD, step, 0)

    finish(ahead, cells, ahead_out)
    finish(own, 0, own_out)


def pair_sums(pairs, counts, slab, own, ahead):
    cells = own.shape[1]
    shape = jax.ShapeDtypeStruct((4, cells, 128), f32)
    both = 2 * cells
    return pl.pallas_call(
        pair_kernel,
        out_shape=(shape, shape),
        in_specs=[pl.BlockSpec(memory_space=pltpu.SMEM)] * 3
        + [pl.BlockSpec(memory_space=pltpu.VMEM)]
        + [pl.BlockSpec(memory_space=pltpu.VMEM)] * 2,
        out_specs=[pl.BlockSpec(memory_space=pltpu.VMEM)] * 2,
        scratch_shapes=[
            pltpu.VMEM((cells, 128, DEPTH), bf16),
            pltpu.VMEM((both, 2, DEPTH, 128), bf16),
            pltpu.VMEM((cells, 2, 128, 128), f32),
            pltpu.VMEM((both, 8, 128), f32),
            pltpu.VMEM((both, 2, 16, 128), bf16),
            pltpu.VMEM((both + 1, 16, 128), f32),
            pltpu.VMEM((AHEAD, 2, 128, 128), f32),
        ],
        compiler_params=pltpu.CompilerParams(vmem_limit_bytes=36 << 20),
        cost_estimate=pl.CostEstimate(flops=4 * 10**9, transcendentals=5 * 10**7, bytes_accessed=2 * 10**6),
    )(pairs, counts, slab, pairs, own, ahead)


def shift(array, by):
    peers = lax.axis_size("slab")
    return lax.ppermute(array, "slab", [(i, i + by) for i in range(peers) if 0 <= i + by < peers])


def copies_of(value, step, ways):
    peers = lax.axis_size("slab")
    return tuple(
        lax.ppermute(value, "slab", [(i, (i + m * step) % peers) for i in range(peers)]) for m in range(1, ways)
    )


def per_device(positions, velocity, density, mass, walls, pairs, counts):
    cells = density.shape[0]
    slab = lax.axis_index("slab")
    state = lax.optimization_barrier(jnp.concatenate([positions, velocity, density[None], mass[None]], 0))
    arrived = shift(state, -1)
    speed = jnp.max(jnp.sum(velocity * velocity, axis=0).reshape(-1, 8, 128), axis=0)
    peers = lax.axis_size("slab")
    reach = min(FIRST_WAYS, peers)
    others = copies_of(speed, 1, reach)
    kept, lent = pair_sums(pairs, counts, slab.astype(jnp.int32).reshape(1), state, arrived)
    summed = kept + shift(lent, 1)
    others, _ = lax.optimization_barrier((others, lent))
    speed = functools.reduce(jnp.maximum, others, speed)
    while reach < peers:
        ways = min(LATER_WAYS, -(-peers // reach))
        speed = functools.reduce(jnp.maximum, copies_of(speed, reach, ways), speed)
        reach *= ways
    fastest = jnp.max(speed)
    step_size = CFL_NUMBER * SMOOTH / (SOUND + jnp.sqrt(fastest))
    gravity = jnp.array([0.0, 0.0, -9.81], f32)[:, None, None]
    fluid = (walls == 0)[None]
    new_velocity = jnp.where(fluid, state[3:6] + step_size * (summed[:3] + gravity), state[3:6])
    within = jnp.arange(cells, dtype=jnp.int32)
    corner = jnp.stack(
        [
            jnp.zeros((cells,), f32) + slab.astype(f32),
            (within // GZ).astype(f32),
            (within % GZ).astype(f32),
        ]
    )[:, :, None]
    offsets = state[:3] - corner
    new_offsets = jnp.where(fluid, offsets + step_size * new_velocity, offsets)
    new_density = state[6] + step_size * summed[3]
    return (new_offsets, new_velocity, new_density)


def solution(mesh):
    wide = P(None, ("runs", "slab"), None)
    flat = P(("runs", "slab"), None)
    return jax.shard_map(
        per_device,
        mesh=mesh,
        in_specs=(wide, wide, flat, flat, flat, P(None, ("runs", "slab")), P(("runs", "slab"))),
        out_specs=(wide, wide, flat),
        check_vma=False,
    )
```

```python
import functools
import math

import jax
import jax.numpy as jnp
from jax import lax
from jax.experimental import pallas as pl
from jax.experimental.pallas import tpu as pltpu
from jax.sharding import PartitionSpec as P

GY = 8
GZ = 16
SMOOTH = 0.5
SOUND = 10.0
CFL_NUMBER = 0.25
GRAD_SCALE = -105.0 / (16.0 * math.pi * SMOOTH**5)
ETA = 0.01 * SMOOTH * SMOOTH
TINY = 1e-12
DEPTH = 48
GROUP = 44
AHEAD = 4
BUILD = 8
WAYS = 4
bf16 = jnp.bfloat16
f32 = jnp.float32


def split3(value):
    first = value.astype(bf16).astype(f32)
    rest = value - first
    second = rest.astype(bf16).astype(f32)
    third = (rest - second).astype(bf16).astype(f32)
    return first, second, third


def tait_pressure(density):
    square = density * density
    return SOUND * SOUND / 7.0 * (square * square * square * density - 1.0)


def dot_rows(left, right):
    return lax.dot_general(left, right, (((1,), (0,)), ((), ())), preferred_element_type=f32)


def dot_lanes(left, right):
    return lax.dot_general(left, right, (((1,), (1,)), ((), ())), preferred_element_type=f32)


def spread(row, count):
    return jnp.broadcast_to(row, (count, row.shape[1]))


def rows_of(values):
    row = lax.broadcasted_iota(jnp.int32, (8, 128), 0)
    out = jnp.zeros((8, 128), f32)
    for at, value in enumerate(values):
        if value:
            out = jnp.where(row == at, value, out)
    return out


def centred(source, local, corner_x):
    row = lax.broadcasted_iota(jnp.int32, (8, 128), 0)
    middle = jnp.where(row == 0, corner_x, jnp.where(row == 1, 0.5 * GY, jnp.where(row == 2, 0.5 * GZ, 0.0)))
    return source[:, local, :] - middle


def build_cell(cell, local, source, corner_x, as_home, tables):
    home_tab, away_tab, side_tab, row_tab, weight_tab = tables
    row = lax.broadcasted_iota(jnp.int32, (8, 128), 0)
    state = centred(source, local, corner_x)
    x, y, z, vx, vy, vz, rho, mass = [state[k : k + 1] for k in range(8)]
    square = spread(x * x + y * y + z * z, 8)
    along = spread(x * vx + y * vy + z * vz, 8)
    full = jnp.where(row < 6, state, jnp.where(row == 6, square, along))
    parts = split3(full)
    turned = jnp.where(row < 3, pltpu.roll(state, 5, 0), jnp.where(row < 6, pltpu.roll(state, 3, 0), along))
    swapped = split3(turned * rows_of([0.5] * 6 + [-0.5]))
    scale = rows_of([-2.0] * 3 + [0.0] * 3 + [1.0])
    scale_low = rows_of([-2.0] * 3)
    unit = rows_of([0.0] * 6 + [1.0])
    minus = rows_of([0.0] * 7 + [-0.5])
    own_terms = [(0, 0), (1, 1), (2, 0)]
    plain_terms = [(0, 1), (0, 2), (1, 0)]
    held = [jnp.where(row < 6, parts[p], unit) for p in range(2)]
    home_rows = [parts[p] for p, _ in own_terms] + [held[p] for p, _ in plain_terms]
    dist_rows = [parts[q] * scale_low + unit for _, q in own_terms] + [parts[q] * scale for _, q in plain_terms]
    close_rows = [jnp.where(row < 6, swapped[q], minus) for _, q in own_terms] + [swapped[q] for _, q in plain_terms]
    away_tab[cell, 0] = jnp.concatenate(dist_rows, 0).astype(bf16)
    away_tab[cell, 1] = jnp.concatenate(close_rows, 0).astype(bf16)
    dense = spread(20.0 * rho, 8)
    side = jnp.where(row == 0, dense - 20.0, jnp.where(row == 1, spread(tait_pressure(rho), 8), dense + 20.0))
    row_tab[cell] = side
    if as_home:
        side_parts = split3(side)
        columns = jnp.transpose(jnp.concatenate(home_rows + list(side_parts) + [side_parts[0]], 0)).astype(bf16)
        home_tab[local] = columns[:, :DEPTH]
        pick = lax.broadcasted_iota(jnp.int32, (DEPTH + 32, 256), 0)
        half = lax.broadcasted_iota(jnp.int32, (DEPTH + 32, 256), 1) // 128
        chosen = (pick >= DEPTH) & (pick < DEPTH + 24) & (pick % 8 == half)
        wide = dot_rows(columns, jnp.where(chosen, 1.0, 0.0).astype(bf16))
        side_tab[local, 0] = wide[:, :128]
        side_tab[local, 1] = wide[:, 128:]
    volume = spread(GRAD_SCALE * mass / rho, 8)
    factor = jnp.where(row == 0, 1.0, jnp.where(row == 4, -1.0 / 20.0, pltpu.roll(state, 1, 0)))
    first, second, third = split3(volume * factor)
    none = jnp.zeros((8, 128), f32)
    push_low = jnp.where(row < 4, first, pltpu.roll(third, 4, 0))
    push_high = jnp.where(row < 4, second, 0.0)
    rate_high = jnp.where(row == 4, first, jnp.where(row == 5, pltpu.roll(second, 1, 0), 0.0))
    weight_tab[cell, 0] = jnp.concatenate([push_low, push_high], 0).astype(bf16)
    weight_tab[cell, 1] = jnp.concatenate([none, rate_high], 0).astype(bf16)


def pair_kernel(
    pairs_ref, count_ref, slab_ref, pairs_vec, own, ahead, own_out, ahead_out,
    home_tab, away_tab, side_tab, row_tab, weight_tab, sums, products,
):
    cells = own.shape[1]
    slots = pairs_ref.shape[1]
    tables = (home_tab, away_tab, side_tab, row_tab, weight_tab)
    corner_x = slab_ref[0].astype(f32) + 1.0
    count = count_ref[0]

    def home_of(k):
        at = jnp.minimum(k, slots - 1)
        return jnp.minimum(pairs_ref[0, at], pairs_ref[1, at])

    def away_of(k):
        at = jnp.minimum(k, slots - 1)
        return jnp.maximum(pairs_ref[0, at], pairs_ref[1, at])

    def build(source, offset, as_home):
        def step(at, carry):
            for inner in range(BUILD):
                local = at * BUILD + inner
                build_cell(offset + local, local, source, corner_x, as_home, tables)
            return carry

        lax.fori_loop(0, cells // BUILD, step, 0)

    sums[...] = jnp.zeros_like(sums)
    listed = lax.broadcasted_iota(jnp.int32, (1, slots), 1) < count
    lowest = jnp.minimum(pairs_vec[0:1, :], pairs_vec[1:2, :])
    ahead_homes = jnp.max(jnp.where(listed, lowest, 0)) >= cells
    build(own, 0, True)

    build(ahead, cells, False)

    def slot_of(k, base):
        return jnp.clip(home_of(k) - base, 0, cells - 1)

    def form(k, slot, base):
        j = away_of(k)
        both = dot_rows(home_tab[slot_of(k, base)], jnp.concatenate([away_tab[j, 0], away_tab[j, 1]], 1))
        products[slot, 0] = both[:, :128]
        products[slot, 1] = both[:, 128:]

    def factors(k, slot, base):
        i = slot_of(k, base)
        j = away_of(k)
        dist_sq = jnp.maximum(products[slot, 0], TINY)
        closing = products[slot, 1]
        density_b, pressure_b, raised_b = row_tab[j, 0:1], row_tab[j, 1:2], row_tab[j, 2:3]
        density_a = side_tab[i, 0]
        shell = jnp.maximum(1.0 - dist_sq * lax.rsqrt(dist_sq), 0.0)
        cube = shell * shell * shell
        approach = closing * (density_a + raised_b)
        push = (cube * ((side_tab[i, 1] + pressure_b) + jnp.maximum(approach, 0.0))).astype(bf16)
        dist_n, cube_n = dist_sq.astype(bf16), cube.astype(bf16)
        approach_n, closing_n = approach.astype(bf16), closing.astype(bf16)
        shape = dist_n / (dist_n + bf16(ETA))
        skew = (density_b.astype(bf16) - density_a.astype(bf16)) * (shape + closing_n)
        return push, cube_n * (approach_n - skew), cube_n * (approach_n + skew)

    def gather(k, values, base):
        push, rate_home, rate_away = values
        i = home_of(k)
        j = away_of(k)
        to_home = dot_lanes(
            jnp.concatenate([weight_tab[j, 0], weight_tab[j, 1]], 1), jnp.concatenate([push, rate_home], 1)
        )
        to_away = dot_rows(
            jnp.concatenate([weight_tab[i, 0], weight_tab[i, 1]], 1), jnp.concatenate([push, rate_away], 0)
        )
        spare = 2 * cells
        live = (k < count) & (i >= base) & (i < base + cells)
        sums[jnp.where(live, i, spare)] += to_home
        sums[jnp.where(live & (i != j), j, spare)] += to_away

    def sweep(at_pass, carry):
        base = at_pass * cells

        @pl.when(at_pass > 0)
        def _():
            build(ahead, cells, True)

        for k in range(AHEAD - 1):
            form(k, k, base)

        def turn(at, inner_carry):
            held = None
            for inner in range(GROUP):
                k = at * GROUP + inner
                form(k + AHEAD - 1, (inner + AHEAD - 1) % AHEAD, base)
                values = factors(k, inner % AHEAD, base)
                if inner:
                    gather(k - 1, held, base)
                held = values
            gather(at * GROUP + GROUP - 1, held, base)
            return inner_carry

        lax.fori_loop(0, (count + GROUP - 1) // GROUP, turn, 0)
        return carry

    lax.fori_loop(0, jnp.where(ahead_homes, 2, 1), sweep, 0)

    def finish(source, offset, out):
        def step(at, carry):
            for inner in range(BUILD):
                local = at * BUILD + inner
                low, high = sums[offset + local, 0:8], sums[offset + local, 8:16]
                state = centred(source, local, corner_x)
                total = low + pltpu.roll(low, 4, 0) + high
                force = (total - pltpu.roll(state, 1, 0) * spread(total[0:1], 8)) / spread(state[6:7], 8)
                for k in range(3):
                    out[k, pl.ds(local, 1), :] = force[k + 1 : k + 2]
                out[3, pl.ds(local, 1), :] = high[4:5] + high[5:6]
            return carry

        lax.fori_loop(0, cells // BUILD, step, 0)

    finish(ahead, cells, ahead_out)
    finish(own, 0, own_out)


def pair_sums(pairs, counts, slab, own, ahead):
    cells = own.shape[1]
    shape = jax.ShapeDtypeStruct((4, cells, 128), f32)
    both = 2 * cells
    return pl.pallas_call(
        pair_kernel,
        out_shape=(shape, shape),
        in_specs=[pl.BlockSpec(memory_space=pltpu.SMEM)] * 3
        + [pl.BlockSpec(memory_space=pltpu.VMEM)]
        + [pl.BlockSpec(memory_space=pltpu.VMEM)] * 2,
        out_specs=[pl.BlockSpec(memory_space=pltpu.VMEM)] * 2,
        scratch_shapes=[
            pltpu.VMEM((cells, 128, DEPTH), bf16),
            pltpu.VMEM((both, 2, DEPTH, 128), bf16),
            pltpu.VMEM((cells, 2, 128, 128), f32),
            pltpu.VMEM((both, 8, 128), f32),
            pltpu.VMEM((both, 2, 16, 128), bf16),
            pltpu.VMEM((both + 1, 16, 128), f32),
            pltpu.VMEM((AHEAD, 2, 128, 128), f32),
        ],
        compiler_params=pltpu.CompilerParams(vmem_limit_bytes=36 << 20),
        cost_estimate=pl.CostEstimate(flops=4 * 10**9, transcendentals=5 * 10**7, bytes_accessed=2 * 10**6),
    )(pairs, counts, slab, pairs, own, ahead)


def shift(array, by):
    peers = lax.axis_size("slab")
    return lax.ppermute(array, "slab", [(i, i + by) for i in range(peers) if 0 <= i + by < peers])


def copies_of(value, step, ways):
    peers = lax.axis_size("slab")
    return tuple(
        lax.ppermute(value, "slab", [(i, (i + m * step) % peers) for i in range(peers)]) for m in range(1, ways)
    )


def per_device(positions, velocity, density, mass, walls, pairs, counts):
    cells = density.shape[0]
    slab = lax.axis_index("slab")
    state = lax.optimization_barrier(jnp.concatenate([positions, velocity, density[None], mass[None]], 0))
    arrived = shift(state, -1)
    speed = jnp.max(jnp.sum(velocity * velocity, axis=0).reshape(-1, 8, 128), axis=0)
    peers = lax.axis_size("slab")
    reach = min(WAYS, peers)
    others = copies_of(speed, 1, reach)
    kept, lent = pair_sums(pairs, counts, slab.astype(jnp.int32).reshape(1), state, arrived)
    summed = kept + shift(lent, 1)
    others, _ = lax.optimization_barrier((others, lent))
    speed = functools.reduce(jnp.maximum, others, speed)
    while reach < peers:
        ways = min(WAYS, -(-peers // reach))
        speed = functools.reduce(jnp.maximum, copies_of(speed, reach, ways), speed)
        reach *= ways
    fastest = jnp.max(speed)
    step_size = CFL_NUMBER * SMOOTH / (SOUND + jnp.sqrt(fastest))
    gravity = jnp.array([0.0, 0.0, -9.81], f32)[:, None, None]
    fluid = (walls == 0)[None]
    new_velocity = jnp.where(fluid, state[3:6] + step_size * (summed[:3] + gravity), state[3:6])
    within = jnp.arange(cells, dtype=jnp.int32)
    corner = jnp.stack(
        [
            jnp.zeros((cells,), f32) + slab.astype(f32),
            (within // GZ).astype(f32),
            (within % GZ).astype(f32),
        ]
    )[:, :, None]
    offsets = state[:3] - corner
    new_offsets = jnp.where(fluid, offsets + step_size * new_velocity, offsets)
    new_density = state[6] + step_size * summed[3]
    return (new_offsets, new_velocity, new_density)


def solution(mesh):
    wide = P(None, ("runs", "slab"), None)
    flat = P(("runs", "slab"), None)
    return jax.shard_map(
        per_device,
        mesh=mesh,
        in_specs=(wide, wide, flat, flat, flat, P(None, ("runs", "slab")), P(("runs", "slab"))),
        out_specs=(wide, wide, flat),
        check_vma=False,
    )
```

```python
import functools
import math

import jax
import jax.numpy as jnp
from jax import lax
from jax.experimental import pallas as pl
from jax.experimental.pallas import tpu as pltpu
from jax.sharding import PartitionSpec as P

GY = 8
GZ = 16
SMOOTH = 0.5
SOUND = 10.0
CFL_NUMBER = 0.25
GRAD_SCALE = -105.0 / (16.0 * math.pi * SMOOTH**5)
ETA = 0.01 * SMOOTH * SMOOTH
TINY = 1e-12
DEPTH = 48
GROUP = 24
AHEAD = 4
BUILD = 8
WAYS = 4
bf16 = jnp.bfloat16
f32 = jnp.float32


def split3(value):
    first = value.astype(bf16).astype(f32)
    rest = value - first
    second = rest.astype(bf16).astype(f32)
    third = (rest - second).astype(bf16).astype(f32)
    return first, second, third


def tait_pressure(density):
    square = density * density
    return SOUND * SOUND / 7.0 * (square * square * square * density - 1.0)


def dot_rows(left, right):
    return lax.dot_general(left, right, (((1,), (0,)), ((), ())), preferred_element_type=f32)


def dot_lanes(left, right):
    return lax.dot_general(left, right, (((1,), (1,)), ((), ())), preferred_element_type=f32)


def spread(row, count):
    return jnp.broadcast_to(row, (count, row.shape[1]))


def rows_of(values):
    row = lax.broadcasted_iota(jnp.int32, (8, 128), 0)
    out = jnp.zeros((8, 128), f32)
    for at, value in enumerate(values):
        if value:
            out = jnp.where(row == at, value, out)
    return out


def centred(source, local, corner_x):
    row = lax.broadcasted_iota(jnp.int32, (8, 128), 0)
    middle = jnp.where(row == 0, corner_x, jnp.where(row == 1, 0.5 * GY, jnp.where(row == 2, 0.5 * GZ, 0.0)))
    return source[:, local, :] - middle


def build_cell(cell, local, source, corner_x, as_home, tables):
    home_tab, away_tab, side_tab, row_tab, weight_tab = tables
    row = lax.broadcasted_iota(jnp.int32, (8, 128), 0)
    state = centred(source, local, corner_x)
    x, y, z, vx, vy, vz, rho, mass = [state[k : k + 1] for k in range(8)]
    square = spread(x * x + y * y + z * z, 8)
    along = spread(x * vx + y * vy + z * vz, 8)
    full = jnp.where(row < 6, state, jnp.where(row == 6, square, along))
    parts = split3(full)
    turned = jnp.where(row < 3, pltpu.roll(state, 5, 0), jnp.where(row < 6, pltpu.roll(state, 3, 0), along))
    swapped = split3(turned * rows_of([0.5] * 6 + [-0.5]))
    scale = rows_of([-2.0] * 3 + [0.0] * 3 + [1.0])
    scale_low = rows_of([-2.0] * 3)
    unit = rows_of([0.0] * 6 + [1.0])
    minus = rows_of([0.0] * 7 + [-0.5])
    own_terms = [(0, 0), (1, 1), (2, 0)]
    plain_terms = [(0, 1), (0, 2), (1, 0)]
    held = [jnp.where(row < 6, parts[p], unit) for p in range(2)]
    home_rows = [parts[p] for p, _ in own_terms] + [held[p] for p, _ in plain_terms]
    dist_rows = [parts[q] * scale_low + unit for _, q in own_terms] + [parts[q] * scale for _, q in plain_terms]
    close_rows = [jnp.where(row < 6, swapped[q], minus) for _, q in own_terms] + [swapped[q] for _, q in plain_terms]
    away_tab[cell, 0] = jnp.concatenate(dist_rows, 0).astype(bf16)
    away_tab[cell, 1] = jnp.concatenate(close_rows, 0).astype(bf16)
    dense = spread(20.0 * rho, 8)
    side = jnp.where(row == 0, dense - 20.0, jnp.where(row == 1, spread(tait_pressure(rho), 8), dense + 20.0))
    row_tab[cell] = side
    if as_home:
        side_parts = split3(side)
        columns = jnp.transpose(jnp.concatenate(home_rows + list(side_parts) + [side_parts[0]], 0)).astype(bf16)
        home_tab[local] = columns[:, :DEPTH]
        pick = lax.broadcasted_iota(jnp.int32, (DEPTH + 32, 256), 0)
        half = lax.broadcasted_iota(jnp.int32, (DEPTH + 32, 256), 1) // 128
        chosen = (pick >= DEPTH) & (pick < DEPTH + 24) & (pick % 8 == half)
        wide = dot_rows(columns, jnp.where(chosen, 1.0, 0.0).astype(bf16))
        side_tab[local, 0] = wide[:, :128]
        side_tab[local, 1] = wide[:, 128:]
    volume = spread(GRAD_SCALE * mass / rho, 8)
    factor = jnp.where(row == 0, 1.0, jnp.where(row == 4, -1.0 / 20.0, pltpu.roll(state, 1, 0)))
    first, second, third = split3(volume * factor)
    none = jnp.zeros((8, 128), f32)
    push_low = jnp.where(row < 4, first, pltpu.roll(third, 4, 0))
    push_high = jnp.where(row < 4, second, 0.0)
    rate_high = jnp.where(row == 4, first, jnp.where(row == 5, pltpu.roll(second, 1, 0), 0.0))
    weight_tab[cell, 0] = jnp.concatenate([push_low, push_high], 0).astype(bf16)
    weight_tab[cell, 1] = jnp.concatenate([none, rate_high], 0).astype(bf16)


def pair_kernel(
    pairs_ref, count_ref, slab_ref, pairs_vec, own, ahead, own_out, ahead_out,
    home_tab, away_tab, side_tab, row_tab, weight_tab, sums, products,
):
    cells = own.shape[1]
    slots = pairs_ref.shape[1]
    tables = (home_tab, away_tab, side_tab, row_tab, weight_tab)
    corner_x = slab_ref[0].astype(f32) + 1.0
    count = count_ref[0]

    def home_of(k):
        at = jnp.minimum(k, slots - 1)
        return jnp.minimum(pairs_ref[0, at], pairs_ref[1, at])

    def away_of(k):
        at = jnp.minimum(k, slots - 1)
        return jnp.maximum(pairs_ref[0, at], pairs_ref[1, at])

    def build(source, offset, as_home):
        def step(at, carry):
            for inner in range(BUILD):
                local = at * BUILD + inner
                build_cell(offset + local, local, source, corner_x, as_home, tables)
            return carry

        lax.fori_loop(0, cells // BUILD, step, 0)

    sums[...] = jnp.zeros_like(sums)
    listed = lax.broadcasted_iota(jnp.int32, (1, slots), 1) < count
    lowest = jnp.minimum(pairs_vec[0:1, :], pairs_vec[1:2, :])
    ahead_homes = jnp.max(jnp.where(listed, lowest, 0)) >= cells
    build(own, 0, True)

    build(ahead, cells, False)

    def slot_of(k, base):
        return jnp.clip(home_of(k) - base, 0, cells - 1)

    def form(k, slot, base):
        j = away_of(k)
        both = dot_rows(home_tab[slot_of(k, base)], jnp.concatenate([away_tab[j, 0], away_tab[j, 1]], 1))
        products[slot, 0] = both[:, :128]
        products[slot, 1] = both[:, 128:]

    def factors(k, slot, base):
        i = slot_of(k, base)
        j = away_of(k)
        dist_sq = jnp.maximum(products[slot, 0], TINY)
        closing = products[slot, 1]
        density_b, pressure_b, raised_b = row_tab[j, 0:1], row_tab[j, 1:2], row_tab[j, 2:3]
        density_a = side_tab[i, 0]
        shell = jnp.maximum(1.0 - dist_sq * lax.rsqrt(dist_sq), 0.0)
        cube = shell * shell * shell
        approach = closing * (density_a + raised_b)
        push = (cube * ((side_tab[i, 1] + pressure_b) + jnp.maximum(approach, 0.0))).astype(bf16)
        dist_n, cube_n = dist_sq.astype(bf16), cube.astype(bf16)
        approach_n, closing_n = approach.astype(bf16), closing.astype(bf16)
        shape = dist_n / (dist_n + bf16(ETA))
        skew = (density_b.astype(bf16) - density_a.astype(bf16)) * (shape + closing_n)
        return push, cube_n * (approach_n - skew), cube_n * (approach_n + skew)

    def gather(k, values, base):
        push, rate_home, rate_away = values
        i = home_of(k)
        j = away_of(k)
        to_home = dot_lanes(
            jnp.concatenate([weight_tab[j, 0], weight_tab[j, 1]], 1), jnp.concatenate([push, rate_home], 1)
        )
        to_away = dot_rows(
            jnp.concatenate([weight_tab[i, 0], weight_tab[i, 1]], 1), jnp.concatenate([push, rate_away], 0)
        )
        spare = 2 * cells
        live = (k < count) & (i >= base) & (i < base + cells)
        sums[jnp.where(live, i, spare)] += to_home
        sums[jnp.where(live & (i != j), j, spare)] += to_away

    def sweep(at_pass, carry):
        base = at_pass * cells

        @pl.when(at_pass > 0)
        def _():
            build(ahead, cells, True)

        for k in range(AHEAD - 1):
            form(k, k, base)

        def turn(at, inner_carry):
            held = None
            for inner in range(GROUP):
                k = at * GROUP + inner
                form(k + AHEAD - 1, (inner + AHEAD - 1) % AHEAD, base)
                values = factors(k, inner % AHEAD, base)
                if inner:
                    gather(k - 1, held, base)
                held = values
            gather(at * GROUP + GROUP - 1, held, base)
            return inner_carry

        lax.fori_loop(0, (count + GROUP - 1) // GROUP, turn, 0)
        return carry

    lax.fori_loop(0, jnp.where(ahead_homes, 2, 1), sweep, 0)

    def finish(source, offset, out):
        def step(at, carry):
            for inner in range(BUILD):
                local = at * BUILD + inner
                low, high = sums[offset + local, 0:8], sums[offset + local, 8:16]
                state = centred(source, local, corner_x)
                total = low + pltpu.roll(low, 4, 0) + high
                force = (total - pltpu.roll(state, 1, 0) * spread(total[0:1], 8)) / spread(state[6:7], 8)
                for k in range(3):
                    out[k, pl.ds(local, 1), :] = force[k + 1 : k + 2]
                out[3, pl.ds(local, 1), :] = high[4:5] + high[5:6]
            return carry

        lax.fori_loop(0, cells // BUILD, step, 0)

    finish(ahead, cells, ahead_out)
    finish(own, 0, own_out)


def pair_sums(pairs, counts, slab, own, ahead):
    cells = own.shape[1]
    shape = jax.ShapeDtypeStruct((4, cells, 128), f32)
    both = 2 * cells
    return pl.pallas_call(
        pair_kernel,
        out_shape=(shape, shape),
        in_specs=[pl.BlockSpec(memory_space=pltpu.SMEM)] * 3
        + [pl.BlockSpec(memory_space=pltpu.VMEM)]
        + [pl.BlockSpec(memory_space=pltpu.VMEM)] * 2,
        out_specs=[pl.BlockSpec(memory_space=pltpu.VMEM)] * 2,
        scratch_shapes=[
            pltpu.VMEM((cells, 128, DEPTH), bf16),
            pltpu.VMEM((both, 2, DEPTH, 128), bf16),
            pltpu.VMEM((cells, 2, 128, 128), f32),
            pltpu.VMEM((both, 8, 128), f32),
            pltpu.VMEM((both, 2, 16, 128), bf16),
            pltpu.VMEM((both + 1, 16, 128), f32),
            pltpu.VMEM((AHEAD, 2, 128, 128), f32),
        ],
        compiler_params=pltpu.CompilerParams(vmem_limit_bytes=36 << 20),
        cost_estimate=pl.CostEstimate(flops=4 * 10**9, transcendentals=5 * 10**7, bytes_accessed=2 * 10**6),
    )(pairs, counts, slab, pairs, own, ahead)


def shift(array, by):
    peers = lax.axis_size("slab")
    return lax.ppermute(array, "slab", [(i, i + by) for i in range(peers) if 0 <= i + by < peers])


def copies_of(value, step, ways):
    peers = lax.axis_size("slab")
    return tuple(
        lax.ppermute(value, "slab", [(i, (i + m * step) % peers) for i in range(peers)]) for m in range(1, ways)
    )


def per_device(positions, velocity, density, mass, walls, pairs, counts):
    cells = density.shape[0]
    slab = lax.axis_index("slab")
    state = lax.optimization_barrier(jnp.concatenate([positions, velocity, density[None], mass[None]], 0))
    arrived = shift(state, -1)
    speed = jnp.max(jnp.sum(velocity * velocity, axis=0).reshape(-1, 8, 128), axis=0)
    peers = lax.axis_size("slab")
    reach = min(WAYS, peers)
    others = copies_of(speed, 1, reach)
    kept, lent = pair_sums(pairs, counts, slab.astype(jnp.int32).reshape(1), state, arrived)
    summed = kept + shift(lent, 1)
    others, _ = lax.optimization_barrier((others, lent))
    speed = functools.reduce(jnp.maximum, others, speed)
    while reach < peers:
        ways = min(WAYS, -(-peers // reach))
        speed = functools.reduce(jnp.maximum, copies_of(speed, reach, ways), speed)
        reach *= ways
    fastest = jnp.max(speed)
    step_size = CFL_NUMBER * SMOOTH / (SOUND + jnp.sqrt(fastest))
    gravity = jnp.array([0.0, 0.0, -9.81], f32)[:, None, None]
    fluid = (walls == 0)[None]
    new_velocity = jnp.where(fluid, state[3:6] + step_size * (summed[:3] + gravity), state[3:6])
    within = jnp.arange(cells, dtype=jnp.int32)
    corner = jnp.stack(
        [
            jnp.zeros((cells,), f32) + slab.astype(f32),
            (within // GZ).astype(f32),
            (within % GZ).astype(f32),
        ]
    )[:, :, None]
    offsets = state[:3] - corner
    new_offsets = jnp.where(fluid, offsets + step_size * new_velocity, offsets)
    new_density = state[6] + step_size * summed[3]
    return (new_offsets, new_velocity, new_density)


def solution(mesh):
    wide = P(None, ("runs", "slab"), None)
    flat = P(("runs", "slab"), None)
    return jax.shard_map(
        per_device,
        mesh=mesh,
        in_specs=(wide, wide, flat, flat, flat, P(None, ("runs", "slab")), P(("runs", "slab"))),
        out_specs=(wide, wide, flat),
        check_vma=False,
    )
```
